32 devices in a mesh: row: 8 (over y, x, core), col: 4 (over z).
Axes of the slice: x: 2, y: 2, z: 4, core: 2. Of those that a mesh axis runs over, the one named last changes fastest.
Arguments:
- start_vector: float32 [131072], P(('row', 'col'))
- energies: float32 [131072], P(('row', 'col')), may hold values from 0.5 to 4
- tile_values: float32 [8, 1024, 4096], P('row', 'col'), may hold values from -0.375 to 0.375
- tile_rows: int32 [8, 1024], P('row', 'col'), may hold values from 0 to 255, as said below
- tile_cols: int32 [8, 1024], P('row', 'col'), may hold values from 0 to 511, as said below
- tile_counts: int32 [8, 4], P('row', 'col'), may hold values from 1 to 256, as said below
Outputs:
- lanczos_vector: float32 [131072], P(('row', 'col'))
- alphas: float32 [2], replicated
- betas: float32 [2], replicated
The draws below stay inside these ranges and needn't reach their ends.
Inputs may be any that keep to these rules, and one draw needn't show every extreme that they name: `tile_rows`: every slot's global tile row is at least its global tile column; each local tile row is below 4 * 64. `tile_cols`: each local tile column is below 8 * 64. `tile_counts`: at most 256 live slots on a device, reached on some device in every draw.
All inputs are finite; a program needn't handle non-finite values.
Results may differ from the reference program's by a relative error of at most 0.00016.
Values sent between devices are 32-bit elements; how exact they have to be, the bound alone decides.
A program may use at most 128 MiB of HBM per device.

```python
import math
import jax
import jax.numpy as jnp
from jax import lax

TILE = 64
PIECE = 4096
NNZT = 256
STEPS = 2
DIM = 131072
N_ROW = 8
N_COL = 4


def occupancy(key):
    per_tile = PIECE // TILE
    row_ids = jnp.arange(N_ROW, dtype=jnp.int32)[:, None, None]
    col_ids = jnp.arange(N_COL, dtype=jnp.int32)[None, :, None]
    pair_count = row_ids * N_COL + N_COL - col_ids
    keys = jax.random.split(jax.random.fold_in(key, 7), 4)
    shape_all = (N_ROW, N_COL, NNZT)
    choose = jax.random.randint(keys[0], shape_all, 0, 1 << 30) % pair_count
    below = choose < row_ids * N_COL
    source_row = jnp.where(below, choose // N_COL, row_ids)
    target_col = jnp.where(below, choose % N_COL, col_ids + (choose - row_ids * N_COL))
    inner_row = jax.random.randint(keys[1], shape_all, 0, per_tile)
    inner_col = jax.random.randint(keys[2], shape_all, 0, per_tile)
    on_diag = jnp.logical_and(jnp.logical_not(below), target_col == col_ids)
    upper_pick = jnp.where(on_diag, jnp.maximum(inner_row, inner_col), inner_row)
    lower_pick = jnp.where(on_diag, jnp.minimum(inner_row, inner_col), inner_col)
    local_rows = (target_col * per_tile + upper_pick).astype(jnp.int32)
    local_cols = (source_row * per_tile + lower_pick).astype(jnp.int32)
    base_count = NNZT * pair_count[:, :, 0] // (N_ROW * N_COL)
    reduction = jax.random.randint(keys[3], (N_ROW, N_COL), 0, NNZT // 8 + 1)
    counts = jnp.maximum(1, base_count - reduction)
    counts = counts.at[N_ROW - 1, 0].set(NNZT).astype(jnp.int32)
    return (local_rows.reshape(N_ROW, N_COL * NNZT), local_cols.reshape(N_ROW, N_COL * NNZT), counts)


def draw_tile_rows(key, part):
    return occupancy(key)[0]


def draw_tile_cols(key, part):
    return occupancy(key)[1]


def draw_tile_counts(key, part):
    return occupancy(key)[2]


def draw_start_vector(key, part):
    piece_ids = (jnp.arange(DIM) // PIECE).astype(jnp.float32)
    rising = 1.0 + 2.0 * piece_ids / max(N_ROW * N_COL - 1, 1)
    keys = jax.random.split(key, 1)
    values = jax.random.normal(keys[0], (DIM,), jnp.float32)
    return (values * rising).astype(jnp.float32)


def block_scale(rng, shape, shards, least, top_value):
    factor_of = 1.0
    for axis_at, parts in shards:
        heights = jax.random.uniform(jax.random.fold_in(jax.random.fold_in(rng, 6), axis_at), (parts,), jnp.float32, least / len(shards), top_value / len(shards))
        factor_of = factor_of * jnp.repeat(jnp.exp(heights), shape[axis_at] // parts).reshape((-1,) + (1,) * (len(shape) - 1 - axis_at))
    return factor_of


def noise(own_key, extent, deviation, bound, shards=(), held_as=jnp.bfloat16):
    values = jax.random.normal(own_key, extent, jnp.float32) * deviation
    if len(shards) > 0:
        values = block_scale(own_key, extent, shards, -0.22, 0.18) * values
    return jnp.clip(values, min=-bound, max=bound).astype(held_as)


def setup_inputs(seed: int = 0) -> dict:
    key_list = jax.random.split(jax.random.key(seed), 7)
    return {
        "start_vector": draw_start_vector(jax.random.fold_in(key_list[6], 71), 0),
        "energies": jnp.clip(jnp.exp(math.log(4.0) - 2.0794415 * jax.random.uniform(key_list[1], (DIM,), jnp.float32) ** block_scale(key_list[1], (DIM,), ((0, 32),), -0.2, 0.2)), 0.5, 4.0),
        "tile_values": noise(key_list[2], (N_ROW, N_COL * NNZT, TILE * TILE), (NNZT * TILE * TILE // PIECE) ** -0.5, 0.375, ((0, 8), (1, 4)), jnp.float32),
        "tile_rows": draw_tile_rows(jax.random.fold_in(key_list[6], 71), 0),
        "tile_cols": draw_tile_cols(jax.random.fold_in(key_list[6], 71), 0),
        "tile_counts": draw_tile_counts(jax.random.fold_in(key_list[6], 71), 0),
    }


def reference(start_vector, energies, tile_values, tile_rows, tile_cols, tile_counts):
    per_tile = PIECE // TILE
    row_ids = jnp.arange(N_ROW, dtype=jnp.int32)[:, None, None]
    col_ids = jnp.arange(N_COL, dtype=jnp.int32)[None, :, None]
    slot_ids = jnp.arange(NNZT, dtype=jnp.int32)[None, None, :]
    local_rows = tile_rows.reshape(N_ROW, N_COL, NNZT)
    local_cols = tile_cols.reshape(N_ROW, N_COL, NNZT)
    global_rows = ((row_ids * N_COL + local_rows // per_tile) * per_tile + local_rows % per_tile).reshape(-1).astype(jnp.int32)
    global_cols = ((local_cols // per_tile * N_COL + col_ids) * per_tile + local_cols % per_tile).reshape(-1).astype(jnp.int32)
    live_mask = (slot_ids < tile_counts[:, :, None]).astype(jnp.float32).reshape(-1)
    blocks = tile_values.reshape(-1, TILE, TILE)

    def apply(vector):
        pieces = vector.reshape(-1, TILE)
        direct = jnp.einsum('kab,kb->ka', blocks, pieces[global_cols], precision=lax.Precision.HIGHEST) * live_mask[:, None]
        mirror = jnp.einsum('kab,ka->kb', blocks, pieces[global_rows], precision=lax.Precision.HIGHEST) * live_mask[:, None]
        result = jnp.zeros((DIM // TILE, TILE), jnp.float32).at[global_rows].add(direct).at[global_cols].add(mirror)
        return result.reshape(-1) + energies * vector
    vector = start_vector / jnp.sqrt(jnp.sum(start_vector * start_vector) / DIM + 1e-06)
    previous = jnp.zeros_like(vector)
    beta_now = jnp.float32(0.0)
    alpha_list = []
    beta_list = []
    for iteration in range(STEPS):
        work = apply(vector) - beta_now * previous
        alpha_now = jnp.sum(vector * work) / DIM
        work = work - alpha_now * vector
        beta_now = jnp.sqrt(jnp.sum(work * work) / DIM + 1e-06)
        previous = vector
        vector = work / beta_now
        alpha_list.append(alpha_now)
        beta_list.append(beta_now)
    return (vector, jnp.stack(alpha_list).astype(jnp.float32), jnp.stack(beta_list).astype(jnp.float32))
```

```python
import functools

import jax
import jax.numpy as jnp
from jax import lax
from jax.experimental import pallas as pl
from jax.experimental.pallas import tpu as pltpu
from jax.sharding import PartitionSpec as P

TILE = 64
STEPS = 2
LANES = 128
CHUNK = 256
UNROLL = True
MESH = pl.DeviceIdType.MESH
F32 = jnp.float32
BF16 = jnp.bfloat16


def split2(x):
    hi = x.astype(BF16)
    return hi, (x - hi.astype(F32)).astype(BF16)


def pick(one_hot, x):
    both = jnp.dot(one_hot, jnp.concatenate(split2(x), axis=1), preferred_element_type=F32)
    return both[:, :LANES] + both[:, LANES:]


def flipped(me, bits, size):
    out, step = me * 0, 1
    while step < size:
        out += ((me // step + bits // step) % 2) * step
        step *= 2
    return out


def peers_of(me, size):
    if size & (size - 1):
        return [lax.rem(me + o, size) for o in range(1, size)]
    return [flipped(me, bits, size) for bits in range(size - 1, 0, -1)]


def kernel(
    n_row, n_col, total,
    s_hbm, e_hbm, t_hbm, tr_hbm, tc_hbm, cnt_hbm,
    out_ref,
    s_ref, e_ref, tr_ref, tc_ref, cnt_ref, t_ref, w_ref, rowbuf, colbuf, dfull, mfull, drecv, mrecv,
    pay, s1buf, s2buf, paya, buf3,
    oc, orr, oct_, ort, ssum, sexp, xc2, xk, accd, accm, mr_ref, mc_ref,
    in_sem, gc_s, gc_r, gr_s, gr_r, rd_s, rd_r, rm_s, rm_r,
    a1_s, a1_r, a2_s, a2_r, a3_s, a3_r,
):
    r = lax.axis_index("row")
    c = lax.axis_index("col")
    pr = s_ref.shape[0]
    slots = t_ref.shape[0]
    flat = t_ref.shape[1]
    chunks = flat // CHUNK

    load_s, load_tr, load_tc, load_cnt, load_e, load_t = loads = [
        pltpu.make_async_copy(src, dst, in_sem.at[i])
        for i, (src, dst) in enumerate([
            (s_hbm, s_ref), (tr_hbm, tr_ref), (tc_hbm, tc_ref),
            (cnt_hbm, cnt_ref), (e_hbm, e_ref), (t_hbm, t_ref),
        ])
    ]
    for d in loads:
        d.start()

    row_peers = peers_of(r, n_row)
    col_peers = peers_of(c, n_col)

    barrier = pltpu.get_barrier_semaphore()
    for p in row_peers:
        pl.semaphore_signal(barrier, inc=1, device_id=(p, c), device_id_type=MESH)
    for p in col_peers:
        pl.semaphore_signal(barrier, inc=1, device_id=(r, p), device_id_type=MESH)
    pl.semaphore_wait(barrier, n_row + n_col - 2)

    def remote(src, dst, ss, rs, dev):
        return pltpu.make_async_remote_copy(
            src_ref=src, dst_ref=dst, send_sem=ss, recv_sem=rs,
            device_id=dev, device_id_type=MESH,
        )

    def slab(p):
        return pl.ds(pl.multiple_of(p * pr, pr), pr)

    sends = []

    def gather(it, src):
        for o, p in enumerate(row_peers):
            d = remote(src, colbuf.at[it, slab(r)], gc_s.at[it, o], gc_r.at[it, r], (p, c))
            d.start()
            sends.append(d)
        for o, p in enumerate(col_peers):
            d = remote(src, rowbuf.at[it, slab(c)], gr_s.at[it, o], gr_r.at[it, c], (r, p))
            d.start()
            sends.append(d)

    def wait_col(it):
        for o, p in enumerate(row_peers):
            remote(colbuf.at[it, slab(p)], colbuf.at[it, slab(p)], gc_s.at[it, o], gc_r.at[it, p], (p, c)).wait_recv()

    def wait_row(it):
        for o, p in enumerate(col_peers):
            remote(rowbuf.at[it, slab(p)], rowbuf.at[it, slab(p)], gr_s.at[it, o], gr_r.at[it, p], (r, p)).wait_recv()

    def scal_one(k):
        for o, p in enumerate(row_peers):
            d = remote(pay.at[k, 0], s1buf.at[k, r], a1_s.at[k, o], a1_r.at[k, r], (p, c))
            d.start()
            sends.append(d)

    def scal_one_get(k):
        parts = [pay[k, 0]]
        for o, p in enumerate(row_peers):
            remote(s1buf.at[k, p], s1buf.at[k, p], a1_s.at[k, o], a1_r.at[k, p], (p, c)).wait_recv()
            parts.append(s1buf[k, p])
        return parts

    def scal_two(k):
        for o, p in enumerate(col_peers):
            d = remote(pay.at[k, 1], s2buf.at[k, c], a2_s.at[k, o], a2_r.at[k, c], (r, p))
            d.start()
            sends.append(d)

    def scal_two_get(k):
        parts = [pay[k, 1]]
        for o, p in enumerate(col_peers):
            remote(s2buf.at[k, p], s2buf.at[k, p], a2_s.at[k, o], a2_r.at[k, p], (r, p)).wait_recv()
            parts.append(s2buf[k, p])
        return parts

    def whole(x):
        return jnp.broadcast_to(jnp.sum(jnp.sum(x, axis=0, keepdims=True), axis=1, keepdims=True), (1, LANES))

    def moments(v, w):
        vw = whole(v * w)
        vv = whole(v * v)
        mean = jnp.where(vv > 0, vw / jnp.where(vv > 0, vv, 1.0), 0.0)
        z = w - mean * v
        return packed(vw, vv, whole(z * z), mean)

    def packed(vw, vv, zz, mean):
        return jnp.concatenate([vw, vv, zz, mean, jnp.zeros((4, LANES), F32)], axis=0)

    def spread_about(parts, center):
        out = jnp.zeros((1, LANES), F32)
        for q in parts:
            gap = center - q[3:4]
            out += q[2:3] + gap * gap * q[1:2]
        return out

    def merge(parts):
        vw = functools.reduce(jnp.add, [q[0:1] for q in parts])
        vv = functools.reduce(jnp.add, [q[1:2] for q in parts])
        mean = jnp.where(vv > 0, vw / jnp.where(vv > 0, vv, 1.0), 0.0)
        return packed(vw, vv, spread_about(parts, mean), mean)

    def alpha_beta(parts):
        vw = functools.reduce(jnp.add, [q[0:1] for q in parts])
        alpha = vw / total
        beta = jnp.sqrt(spread_about(parts, alpha) / total + 1e-06)
        return alpha, beta

    load_s.wait()
    s = s_ref[...]
    gather(0, s_ref)
    colbuf[0, slab(r)] = s
    rowbuf[0, slab(c)] = s
    pay[0, 0] = jnp.broadcast_to(whole(s * s), (8, LANES))
    scal_one(0)

    lane = lax.broadcasted_iota(jnp.int32, (slots, LANES), 1)
    half = lane // TILE
    slot = lax.broadcasted_iota(jnp.int32, (slots, LANES), 0)
    load_cnt.wait()
    load_tr.wait()
    load_tc.wait()
    live = slot < cnt_ref[0, 0]
    a_row = tr_ref[...]
    b_row = tc_ref[...]
    a_col = jnp.transpose(jnp.broadcast_to(a_row, (LANES, slots)))
    b_col = jnp.transpose(jnp.broadcast_to(b_row, (LANES, slots)))

    def as_one(m):
        return jnp.where(m, 1.0, 0.0).astype(F32)

    a_half = as_one((a_col & 1) == half)
    b_half = as_one((b_col & 1) == half)
    alive = as_one(live)
    mr_ref[0] = a_half
    mr_ref[1] = a_half * alive
    mc_ref[0] = b_half
    mc_ref[1] = b_half * alive
    for h in range(orr.shape[1] // LANES):
        orr[:, h * LANES:(h + 1) * LANES] = as_one((a_col >> 1) == lane + h * LANES).astype(BF16)
    for h in range(oc.shape[1] // LANES):
        oc[:, h * LANES:(h + 1) * LANES] = as_one((b_col >> 1) == lane + h * LANES).astype(BF16)
    ort[...] = as_one(jnp.broadcast_to(a_row >> 1, ort.shape) == lax.broadcasted_iota(jnp.int32, ort.shape, 0)).astype(BF16)
    oct_[...] = as_one(jnp.broadcast_to(b_row >> 1, oct_.shape) == lax.broadcasted_iota(jnp.int32, oct_.shape, 0)).astype(BF16)

    k_sum = lax.broadcasted_iota(jnp.int32, (CHUNK, LANES), 0) // TILE
    n_sum = lax.broadcasted_iota(jnp.int32, (CHUNK, LANES), 1) & (TILE - 1)
    k_exp = lax.broadcasted_iota(jnp.int32, (LANES, CHUNK), 0) & (TILE - 1)
    n_exp = lax.broadcasted_iota(jnp.int32, (LANES, CHUNK), 1) // TILE
    per = CHUNK // TILE

    def build(i, carry):
        rows = pl.ds(pl.multiple_of(i * CHUNK, CHUNK), CHUNK)
        ssum[rows, :] = as_one(n_sum == k_sum + i * per).astype(BF16)
        sexp[:, rows] = as_one(k_exp == n_exp + i * per).astype(BF16)
        return carry

    lax.fori_loop(0, chunks, build, 0)

    def twice(x, mask):
        kept = x * mask
        return kept + pltpu.roll(kept, TILE, 1)

    def direct(it):
        x2 = twice(pick(oc[...], colbuf[it]), mc_ref[0])
        xc2[:, :LANES] = x2
        xc2[:, LANES:] = x2
        accd[...] = jnp.zeros_like(accd)

        def step(i, carry):
            cols = pl.ds(pl.multiple_of(i * CHUNK, CHUNK), CHUNK)
            p = t_ref[:, cols] * xc2[...]
            hi = p.astype(BF16)
            lo = (p - hi.astype(F32)).astype(BF16)
            w = ssum[cols, :]
            accd[...] += jnp.dot(hi, w, preferred_element_type=F32) + jnp.dot(lo, w, preferred_element_type=F32)
            return carry

        lax.fori_loop(0, chunks, step, 0, unroll=UNROLL)
        dfull[it] = pick(ort[...], accd[...] * mr_ref[1])
        for o, p in enumerate(col_peers):
            d = remote(dfull.at[it, slab(p)], drecv.at[it, c], rd_s.at[it, o], rd_r.at[it, c], (r, p))
            d.start()
            sends.append(d)

    def mirror(it):
        x2 = twice(pick(orr[...], rowbuf[it]), mr_ref[0])
        hi = x2.astype(BF16).astype(F32)
        xk[...] = jnp.where(half == 0, hi, x2 - hi).astype(BF16)
        accm[...] = jnp.zeros_like(accm)

        def step(i, carry):
            cols = pl.ds(pl.multiple_of(i * CHUNK, CHUNK), CHUNK)
            p = t_ref[:, cols] * jnp.dot(xk[...], sexp[:, cols], preferred_element_type=F32)
            accm[...] += p[:, :LANES] + p[:, LANES:]
            return carry

        lax.fori_loop(0, chunks, step, 0, unroll=UNROLL)
        m = accm[...]
        mfull[it] = pick(oct_[...], (m + pltpu.roll(m, TILE, 1)) * mc_ref[1])
        for o, p in enumerate(row_peers):
            d = remote(mfull.at[it, slab(p)], mrecv.at[it, r], rm_s.at[it, o], rm_r.at[it, r], (p, c))
            d.start()
            sends.append(d)

    def collect(it, x):
        h = e_ref[...] * x + dfull[it, slab(c)] + mfull[it, slab(r)]
        for o, p in enumerate(col_peers):
            remote(drecv.at[it, p], drecv.at[it, p], rd_s.at[it, o], rd_r.at[it, p], (r, p)).wait_recv()
            h += drecv[it, p]
        for o, p in enumerate(row_peers):
            remote(mrecv.at[it, p], mrecv.at[it, p], rm_s.at[it, o], rm_r.at[it, p], (p, c)).wait_recv()
            h += mrecv[it, p]
        return h

    wait_col(0)
    load_t.wait()
    load_e.wait()
    direct(0)
    parts = scal_one_get(0)
    pay[0, 1] = functools.reduce(jnp.add, parts)
    scal_two(0)
    wait_row(0)
    mirror(0)
    square = functools.reduce(jnp.add, scal_two_get(0))[0:1]
    norm = jnp.sqrt(square / total + 1e-06)
    v0 = s / norm
    w0 = collect(0, s) / norm
    w_ref[...] = w0
    gather(1, w_ref)
    colbuf[1, slab(r)] = w0
    rowbuf[1, slab(c)] = w0
    pay[1, 0] = moments(v0, w0)
    scal_one(1)
    wait_col(1)
    direct(1)
    pay[1, 1] = merge(scal_one_get(1))
    scal_two(1)
    wait_row(1)
    mirror(1)
    alpha0, beta0 = alpha_beta(scal_two_get(1))
    v1 = (w0 - alpha0 * v0) / beta0
    w1 = (collect(1, w0) - alpha0 * w0) / beta0 - beta0 * v0
    mine = moments(v1, w1)
    for i in range(4):
        paya[i] = mine[i:i + 1]
    me = r * n_col + c
    count = n_row * n_col
    others = [lax.rem(me + o, count) for o in range(1, count)]
    last = []
    for o, p in enumerate(others):
        d = remote(paya, buf3.at[me], a3_s.at[o], a3_r.at[me], (p // n_col, lax.rem(p, n_col)))
        d.start()
        last.append(d)
    for d in sends:
        d.wait_send()
    sends.clear()
    parts = [(mine[0:1], mine[1:2], mine[2:3], mine[3:4])]
    for o, p in enumerate(others):
        remote(buf3.at[p], buf3.at[p], a3_s.at[o], a3_r.at[p], (p // n_col, lax.rem(p, n_col))).wait_recv()
    for p in others:
        parts.append(tuple(buf3[p, i] for i in range(4)))
    alpha1 = functools.reduce(jnp.add, [q[0] for q in parts]) / total
    spread = functools.reduce(jnp.add, [q[2] + (alpha1 - q[3]) * (alpha1 - q[3]) * q[1] for q in parts])
    beta1 = jnp.sqrt(spread / total + 1e-06)
    out_ref[:pr] = (w1 - alpha1 * v1) / beta1
    at = lax.broadcasted_iota(jnp.int32, (1, LANES), 1)
    out_ref[pr:] = jnp.concatenate(
        [jnp.where(at == 0, alpha0, alpha1), jnp.where(at == 0, beta0, beta1), jnp.zeros((6, LANES), F32)], axis=0
    )
    for d in last:
        d.wait_send()


def hand_out(in_ref, vec_ref, al_ref, be_ref):
    pr = vec_ref.shape[0]
    vec_ref[...] = in_ref[:pr]
    al_ref[...] = in_ref[pr, :STEPS]
    be_ref[...] = in_ref[pr + 1, :STEPS]


def local(start_vector, energies, tile_values, tile_rows, tile_cols, tile_counts):
    n_row = lax.axis_size("row")
    n_col = lax.axis_size("col")
    piece = start_vector.shape[0]
    pr = piece // LANES
    slots, flat = tile_values.shape[1:]
    rr, cr = n_col * pr, n_row * pr
    vm = pl.BlockSpec(memory_space=pltpu.VMEM)
    dma = pltpu.SemaphoreType.DMA
    out = pl.pallas_call(
        functools.partial(kernel, n_row, n_col, float(piece * n_row * n_col)),
        out_shape=pltpu.VMEM((pr + 8, LANES), F32),
        in_specs=[pl.BlockSpec(memory_space=pltpu.HBM)] * 6,
        out_specs=vm,
        scratch_shapes=[
            pltpu.VMEM((pr, LANES), F32),
            pltpu.VMEM((pr, LANES), F32),
            pltpu.VMEM(tile_rows.shape, jnp.int32),
            pltpu.VMEM(tile_cols.shape, jnp.int32),
            pltpu.SMEM(tile_counts.shape, jnp.int32),
            pltpu.VMEM((slots, flat), F32),
            pltpu.VMEM((pr, LANES), F32),
            pltpu.VMEM((2, rr, LANES), F32),
            pltpu.VMEM((2, cr, LANES), F32),
            pltpu.VMEM((2, rr, LANES), F32),
            pltpu.VMEM((2, cr, LANES), F32),
            pltpu.VMEM((2, n_col, pr, LANES), F32),
            pltpu.VMEM((2, n_row, pr, LANES), F32),
            pltpu.VMEM((2, 2, 8, LANES), F32),
            pltpu.VMEM((2, n_row, 8, LANES), F32),
            pltpu.VMEM((2, n_col, 8, LANES), F32),
            pltpu.VMEM((4, 1, LANES), F32),
            pltpu.VMEM((n_row * n_col, 4, 1, LANES), F32),
            pltpu.VMEM((slots, cr), BF16),
            pltpu.VMEM((slots, rr), BF16),
            pltpu.VMEM((cr, slots), BF16),
            pltpu.VMEM((rr, slots), BF16),
            pltpu.VMEM((flat, LANES), BF16),
            pltpu.VMEM((LANES, flat), BF16),
            pltpu.VMEM((slots, CHUNK), F32),
            pltpu.VMEM((slots, LANES), BF16),
            pltpu.VMEM((slots, LANES), F32),
            pltpu.VMEM((slots, LANES), F32),
            pltpu.VMEM((2, slots, LANES), F32),
            pltpu.VMEM((2, slots, LANES), F32),
            dma((6,)),
            dma((2, n_row)), dma((2, n_row)),
            dma((2, n_col)), dma((2, n_col)),
            dma((2, n_col)), dma((2, n_col)),
            dma((2, n_row)), dma((2, n_row)),
            dma((2, n_row)), dma((2, n_row)),
            dma((2, n_col)), dma((2, n_col)),
            dma((n_row * n_col,)), dma((n_row * n_col,)),
        ],
        compiler_params=pltpu.CompilerParams(
            collective_id=0, has_side_effects=True, vmem_limit_bytes=60000000
        ),
    )(
        start_vector.reshape(pr, LANES),
        energies.reshape(pr, LANES),
        tile_values.reshape(slots, flat),
        tile_rows,
        tile_cols,
        tile_counts,
    )
    vector, alphas, betas = pl.pallas_call(
        hand_out,
        out_shape=(
            jax.ShapeDtypeStruct((pr, LANES), F32),
            jax.ShapeDtypeStruct((STEPS,), F32),
            jax.ShapeDtypeStruct((STEPS,), F32),
        ),
        in_specs=[vm],
        out_specs=(vm, vm, vm),
        compiler_params=pltpu.CompilerParams(vmem_limit_bytes=1048576),
    )(out)
    return vector.reshape(piece), alphas, betas


def solution(mesh):
    placed = (
        P(("row", "col")),
        P(("row", "col")),
        P("row", "col", None),
        P("row", "col"),
        P("row", "col"),
        P("row", "col"),
    )
    return jax.shard_map(
        local, mesh=mesh, in_specs=placed, out_specs=(P(("row", "col")), P(), P()), check_vma=False
    )
```

```python
import functools

import jax
import jax.numpy as jnp
from jax import lax
from jax.experimental import pallas as pl
from jax.experimental.pallas import tpu as pltpu
from jax.sharding import PartitionSpec as P

TILE = 64
STEPS = 2
LANES = 128
LOADS = 4
SUBLANES = 8
MESH = pl.DeviceIdType.MESH
F32 = jnp.float32
BF16 = jnp.bfloat16


def split2(x):
    hi = x.astype(BF16)
    return hi, (x - hi.astype(F32)).astype(BF16)


def pick(one_hot, x):
    both = jnp.dot(one_hot, jnp.concatenate(split2(x), axis=1), preferred_element_type=F32)
    return both[:, :LANES] + both[:, LANES:]


def flipped(me, bits, size):
    out, step = me * 0, 1
    while step < size:
        out += ((me // step + bits // step) % 2) * step
        step *= 2
    return out


def peers_of(me, size):
    if size & (size - 1):
        return [lax.rem(me + o, size) for o in range(1, size)]
    return [flipped(me, bits, size) for bits in range(size - 1, 0, -1)]


def kernel(
    n_row, n_col, total,
    s_hbm, e_hbm, t_hbm, tr_hbm, tc_hbm, cnt_hbm,
    out_ref,
    s_ref, e_ref, tr_ref, tc_ref, cnt_ref, t_ref, w_ref, rowbuf, colbuf, dfull, mfull, drecv, mrecv,
    pay, s1buf, s2buf, paya, buf3,
    oc, orr, oct_, ort, tt, xb, xa, dt,
    in_sem, gc_s, gc_r, gr_s, gr_r, rd_s, rd_r, rm_s, rm_r,
    a1_s, a1_r, a2_s, a2_r, a3_s, a3_r,
):
    r = lax.axis_index("row")
    c = lax.axis_index("col")
    pr = s_ref.shape[0]
    slots = t_ref.shape[0]
    flat = t_ref.shape[1]
    part = flat // LOADS

    load_s, load_tr, load_tc, load_cnt, load_e = loads = [
        pltpu.make_async_copy(src, dst, in_sem.at[i])
        for i, (src, dst) in enumerate([
            (s_hbm, s_ref), (tr_hbm, tr_ref), (tc_hbm, tc_ref),
            (cnt_hbm, cnt_ref), (e_hbm, e_ref),
        ])
    ]
    load_t = []
    for i in range(LOADS):
        cols = pl.ds(i * part, part)
        load_t.append(pltpu.make_async_copy(t_hbm.at[:, cols], t_ref.at[:, cols], in_sem.at[len(loads) + i]))
    for d in loads + load_t:
        d.start()

    row_peers = peers_of(r, n_row)
    col_peers = peers_of(c, n_col)

    barrier = pltpu.get_barrier_semaphore()
    for p in row_peers:
        pl.semaphore_signal(barrier, inc=1, device_id=(p, c), device_id_type=MESH)
    for p in col_peers:
        pl.semaphore_signal(barrier, inc=1, device_id=(r, p), device_id_type=MESH)
    pl.semaphore_wait(barrier, n_row + n_col - 2)

    def remote(src, dst, ss, rs, dev):
        return pltpu.make_async_remote_copy(
            src_ref=src, dst_ref=dst, send_sem=ss, recv_sem=rs,
            device_id=dev, device_id_type=MESH,
        )

    def slab(p):
        return pl.ds(pl.multiple_of(p * pr, pr), pr)

    sends = []

    def gather(it, src):
        for o, p in enumerate(row_peers):
            d = remote(src, colbuf.at[it, slab(r)], gc_s.at[it, o], gc_r.at[it, r], (p, c))
            d.start()
            sends.append(d)
        for o, p in enumerate(col_peers):
            d = remote(src, rowbuf.at[it, slab(c)], gr_s.at[it, o], gr_r.at[it, c], (r, p))
            d.start()
            sends.append(d)

    def wait_col(it):
        for o, p in enumerate(row_peers):
            remote(colbuf.at[it, slab(p)], colbuf.at[it, slab(p)], gc_s.at[it, o], gc_r.at[it, p], (p, c)).wait_recv()

    def wait_row(it):
        for o, p in enumerate(col_peers):
            remote(rowbuf.at[it, slab(p)], rowbuf.at[it, slab(p)], gr_s.at[it, o], gr_r.at[it, p], (r, p)).wait_recv()

    def scal_one(k):
        for o, p in enumerate(row_peers):
            d = remote(pay.at[k, 0], s1buf.at[k, r], a1_s.at[k, o], a1_r.at[k, r], (p, c))
            d.start()
            sends.append(d)

    def scal_one_get(k):
        parts = [pay[k, 0]]
        for o, p in enumerate(row_peers):
            remote(s1buf.at[k, p], s1buf.at[k, p], a1_s.at[k, o], a1_r.at[k, p], (p, c)).wait_recv()
            parts.append(s1buf[k, p])
        return parts

    def scal_two(k):
        for o, p in enumerate(col_peers):
            d = remote(pay.at[k, 1], s2buf.at[k, c], a2_s.at[k, o], a2_r.at[k, c], (r, p))
            d.start()
            sends.append(d)

    def scal_two_get(k):
        parts = [pay[k, 1]]
        for o, p in enumerate(col_peers):
            remote(s2buf.at[k, p], s2buf.at[k, p], a2_s.at[k, o], a2_r.at[k, p], (r, p)).wait_recv()
            parts.append(s2buf[k, p])
        return parts

    def whole(x):
        return jnp.broadcast_to(jnp.sum(jnp.sum(x, axis=0, keepdims=True), axis=1, keepdims=True), (1, LANES))

    def moments(v, w):
        vw = whole(v * w)
        vv = whole(v * v)
        mean = jnp.where(vv > 0, vw / jnp.where(vv > 0, vv, 1.0), 0.0)
        z = w - mean * v
        return packed(vw, vv, whole(z * z), mean)

    def packed(vw, vv, zz, mean):
        return jnp.concatenate([vw, vv, zz, mean, jnp.zeros((4, LANES), F32)], axis=0)

    def spread_about(parts, center):
        out = jnp.zeros((1, LANES), F32)
        for q in parts:
            gap = center - q[3:4]
            out += q[2:3] + gap * gap * q[1:2]
        return out

    def merge(parts):
        vw = functools.reduce(jnp.add, [q[0:1] for q in parts])
        vv = functools.reduce(jnp.add, [q[1:2] for q in parts])
        mean = jnp.where(vv > 0, vw / jnp.where(vv > 0, vv, 1.0), 0.0)
        return packed(vw, vv, spread_about(parts, mean), mean)

    def alpha_beta(parts):
        vw = functools.reduce(jnp.add, [q[0:1] for q in parts])
        alpha = vw / total
        beta = jnp.sqrt(spread_about(parts, alpha) / total + 1e-06)
        return alpha, beta

    load_s.wait()
    s = s_ref[...]
    gather(0, s_ref)
    colbuf[0, slab(r)] = s
    rowbuf[0, slab(c)] = s
    pay[0, 0] = jnp.broadcast_to(whole(s * s), (8, LANES))
    scal_one(0)

    lane = lax.broadcasted_iota(jnp.int32, (slots, LANES), 1)
    load_cnt.wait()
    load_tr.wait()
    load_tc.wait()
    live = lax.broadcasted_iota(jnp.int32, (TILE, slots), 1) < cnt_ref[0, 0]
    a_row = tr_ref[...]
    b_row = tc_ref[...]
    a_col = jnp.transpose(jnp.broadcast_to(a_row, (LANES, slots)))
    b_col = jnp.transpose(jnp.broadcast_to(b_row, (LANES, slots)))

    def as_one(m):
        return jnp.where(m, 1.0, 0.0).astype(F32)

    for h in range(orr.shape[1] // LANES):
        orr[:, h * LANES:(h + 1) * LANES] = as_one((a_col >> 1) == lane + h * LANES).astype(BF16)
    for h in range(oc.shape[1] // LANES):
        oc[:, h * LANES:(h + 1) * LANES] = as_one((b_col >> 1) == lane + h * LANES).astype(BF16)
    ort[...] = as_one(jnp.broadcast_to(a_row >> 1, ort.shape) == lax.broadcasted_iota(jnp.int32, ort.shape, 0)).astype(BF16)
    oct_[...] = as_one(jnp.broadcast_to(b_row >> 1, oct_.shape) == lax.broadcasted_iota(jnp.int32, oct_.shape, 0)).astype(BF16)

    a_odd = jnp.broadcast_to(a_row & 1, (TILE, slots)) == 1
    b_odd = jnp.broadcast_to(b_row & 1, (TILE, slots)) == 1

    for i in range(flat // LANES):
        if i * LANES % part == 0:
            load_t[i * LANES // part].wait()
        cols = slice(i * LANES, (i + 1) * LANES)
        tt[cols, :] = jnp.transpose(t_ref[:, cols])

    def gathered(one_hot, x, odd):
        g = jnp.transpose(pick(one_hot, x))
        return jnp.where(odd, g[TILE:], g[:TILE])

    def scattered(one_hot, y, odd):
        zero = jnp.zeros_like(y)
        even_part = jnp.where(odd, zero, jnp.where(live, y, zero))
        odd_part = jnp.where(odd, jnp.where(live, y, zero), zero)
        both = lax.dot_general(
            one_hot, jnp.concatenate(split2(jnp.concatenate([even_part, odd_part], axis=0)), axis=0),
            (((1,), (1,)), ((), ())), preferred_element_type=F32,
        )
        return both[:, :LANES] + both[:, LANES:]

    sub = lax.broadcasted_iota(jnp.int32, (SUBLANES, slots), 0)

    def fold(parts):
        shift = 1
        while len(parts) > 1:
            low = (sub & shift) == 0
            parts = [
                jnp.where(low, p, q) + pltpu.roll(jnp.where(low, q, p), shift, 0)
                for p, q in zip(parts[::2], parts[1::2])
            ]
            shift *= 2
        return parts[0]

    def direct(it):
        xb[...] = gathered(oc[...], colbuf[it], b_odd)
        for g in range(TILE // SUBLANES):
            parts = []
            for a in range(g * SUBLANES, (g + 1) * SUBLANES):
                terms = [
                    tt[a * TILE + q:a * TILE + q + SUBLANES, :] * xb[q:q + SUBLANES, :]
                    for q in range(0, TILE, SUBLANES)
                ]
                parts.append(functools.reduce(jnp.add, terms))
            dt[g * SUBLANES:(g + 1) * SUBLANES, :] = fold(parts)
        dfull[it] = scattered(ort[...], dt[...], a_odd)
        for o, p in enumerate(col_peers):
            d = remote(dfull.at[it, slab(p)], drecv.at[it, c], rd_s.at[it, o], rd_r.at[it, c], (r, p))
            d.start()
            sends.append(d)

    def mirror(it):
        xa[...] = gathered(orr[...], rowbuf[it], a_odd)
        m = jnp.zeros((TILE, slots), F32)
        for a in range(TILE):
            m += tt[a * TILE:(a + 1) * TILE, :] * xa[a:a + 1, :]
        mfull[it] = scattered(oct_[...], m, b_odd)
        for o, p in enumerate(row_peers):
            d = remote(mfull.at[it, slab(p)], mrecv.at[it, r], rm_s.at[it, o], rm_r.at[it, r], (p, c))
            d.start()
            sends.append(d)

    def collect(it, x):
        h = e_ref[...] * x + dfull[it, slab(c)] + mfull[it, slab(r)]
        for o, p in enumerate(col_peers):
            remote(drecv.at[it, p], drecv.at[it, p], rd_s.at[it, o], rd_r.at[it, p], (r, p)).wait_recv()
            h += drecv[it, p]
        for o, p in enumerate(row_peers):
            remote(mrecv.at[it, p], mrecv.at[it, p], rm_s.at[it, o], rm_r.at[it, p], (p, c)).wait_recv()
            h += mrecv[it, p]
        return h

    load_e.wait()
    wait_col(0)
    direct(0)
    parts = scal_one_get(0)
    pay[0, 1] = functools.reduce(jnp.add, parts)
    scal_two(0)
    wait_row(0)
    mirror(0)
    square = functools.reduce(jnp.add, scal_two_get(0))[0:1]
    norm = jnp.sqrt(square / total + 1e-06)
    v0 = s / norm
    w0 = collect(0, s) / norm
    w_ref[...] = w0
    gather(1, w_ref)
    colbuf[1, slab(r)] = w0
    rowbuf[1, slab(c)] = w0
    pay[1, 0] = moments(v0, w0)
    scal_one(1)
    wait_col(1)
    direct(1)
    pay[1, 1] = merge(scal_one_get(1))
    scal_two(1)
    wait_row(1)
    mirror(1)
    alpha0, beta0 = alpha_beta(scal_two_get(1))
    v1 = (w0 - alpha0 * v0) / beta0
    w1 = (collect(1, w0) - alpha0 * w0) / beta0 - beta0 * v0
    mine = moments(v1, w1)
    for i in range(4):
        paya[i] = mine[i:i + 1]
    me = r * n_col + c
    count = n_row * n_col
    others = [lax.rem(me + o, count) for o in range(1, count)]
    last = []
    for o, p in enumerate(others):
        d = remote(paya, buf3.at[me], a3_s.at[o], a3_r.at[me], (p // n_col, lax.rem(p, n_col)))
        d.start()
        last.append(d)
    for d in sends:
        d.wait_send()
    sends.clear()
    parts = [(mine[0:1], mine[1:2], mine[2:3], mine[3:4])]
    for o, p in enumerate(others):
        remote(buf3.at[p], buf3.at[p], a3_s.at[o], a3_r.at[p], (p // n_col, lax.rem(p, n_col))).wait_recv()
    for p in others:
        parts.append(tuple(buf3[p, i] for i in range(4)))
    alpha1 = functools.reduce(jnp.add, [q[0] for q in parts]) / total
    spread = functools.reduce(jnp.add, [q[2] + (alpha1 - q[3]) * (alpha1 - q[3]) * q[1] for q in parts])
    beta1 = jnp.sqrt(spread / total + 1e-06)
    out_ref[:pr] = (w1 - alpha1 * v1) / beta1
    at = lax.broadcasted_iota(jnp.int32, (1, LANES), 1)
    out_ref[pr:] = jnp.concatenate(
        [jnp.where(at == 0, alpha0, alpha1), jnp.where(at == 0, beta0, beta1), jnp.zeros((6, LANES), F32)], axis=0
    )
    for d in last:
        d.wait_send()


def hand_out(in_ref, vec_ref, al_ref, be_ref):
    pr = vec_ref.shape[0]
    vec_ref[...] = in_ref[:pr]
    al_ref[...] = in_ref[pr, :STEPS]
    be_ref[...] = in_ref[pr + 1, :STEPS]


def local(start_vector, energies, tile_values, tile_rows, tile_cols, tile_counts):
    n_row = lax.axis_size("row")
    n_col = lax.axis_size("col")
    piece = start_vector.shape[0]
    pr = piece // LANES
    slots, flat = tile_values.shape[1:]
    rr, cr = n_col * pr, n_row * pr
    vm = pl.BlockSpec(memory_space=pltpu.VMEM)
    dma = pltpu.SemaphoreType.DMA
    out = pl.pallas_call(
        functools.partial(kernel, n_row, n_col, float(piece * n_row * n_col)),
        out_shape=pltpu.VMEM((pr + 8, LANES), F32),
        in_specs=[pl.BlockSpec(memory_space=pltpu.HBM)] * 6,
        out_specs=vm,
        scratch_shapes=[
            pltpu.VMEM((pr, LANES), F32),
            pltpu.VMEM((pr, LANES), F32),
            pltpu.VMEM(tile_rows.shape, jnp.int32),
            pltpu.VMEM(tile_cols.shape, jnp.int32),
            pltpu.SMEM(tile_counts.shape, jnp.int32),
            pltpu.VMEM((slots, flat), F32),
            pltpu.VMEM((pr, LANES), F32),
            pltpu.VMEM((2, rr, LANES), F32),
            pltpu.VMEM((2, cr, LANES), F32),
            pltpu.VMEM((2, rr, LANES), F32),
            pltpu.VMEM((2, cr, LANES), F32),
            pltpu.VMEM((2, n_col, pr, LANES), F32),
            pltpu.VMEM((2, n_row, pr, LANES), F32),
            pltpu.VMEM((2, 2, 8, LANES), F32),
            pltpu.VMEM((2, n_row, 8, LANES), F32),
            pltpu.VMEM((2, n_col, 8, LANES), F32),
            pltpu.VMEM((4, 1, LANES), F32),
            pltpu.VMEM((n_row * n_col, 4, 1, LANES), F32),
            pltpu.VMEM((slots, cr), BF16),
            pltpu.VMEM((slots, rr), BF16),
            pltpu.VMEM((cr, slots), BF16),
            pltpu.VMEM((rr, slots), BF16),
            pltpu.VMEM((flat, slots), F32),
            pltpu.VMEM((TILE, slots), F32),
            pltpu.VMEM((TILE, slots), F32),
            pltpu.VMEM((TILE, slots), F32),
            dma((5 + LOADS,)),
            dma((2, n_row)), dma((2, n_row)),
            dma((2, n_col)), dma((2, n_col)),
            dma((2, n_col)), dma((2, n_col)),
            dma((2, n_row)), dma((2, n_row)),
            dma((2, n_row)), dma((2, n_row)),
            dma((2, n_col)), dma((2, n_col)),
            dma((n_row * n_col,)), dma((n_row * n_col,)),
        ],
        compiler_params=pltpu.CompilerParams(
            collective_id=0, has_side_effects=True, vmem_limit_bytes=60000000
        ),
    )(
        start_vector.reshape(pr, LANES),
        energies.reshape(pr, LANES),
        tile_values.reshape(slots, flat),
        tile_rows,
        tile_cols,
        tile_counts,
    )
    vector, alphas, betas = pl.pallas_call(
        hand_out,
        out_shape=(
            jax.ShapeDtypeStruct((pr, LANES), F32),
            jax.ShapeDtypeStruct((STEPS,), F32),
            jax.ShapeDtypeStruct((STEPS,), F32),
        ),
        in_specs=[vm],
        out_specs=(vm, vm, vm),
        compiler_params=pltpu.CompilerParams(vmem_limit_bytes=1048576),
    )(out)
    return vector.reshape(piece), alphas, betas


def solution(mesh):
    placed = (
        P(("row", "col")),
        P(("row", "col")),
        P("row", "col", None),
        P("row", "col"),
        P("row", "col"),
        P("row", "col"),
    )
    return jax.shard_map(
        local, mesh=mesh, in_specs=placed, out_specs=(P(("row", "col")), P(), P()), check_vma=False
    )
```

```python
import functools

import jax
import jax.numpy as jnp
from jax import lax
from jax.experimental import pallas as pl
from jax.experimental.pallas import tpu as pltpu
from jax.sharding import PartitionSpec as P

TILE = 64
STEPS = 2
LANES = 128
LOADS = 4
SUBLANES = 8
MESH = pl.DeviceIdType.MESH
F32 = jnp.float32
BF16 = jnp.bfloat16


def split2(x):
    hi = x.astype(BF16)
    return hi, (x - hi.astype(F32)).astype(BF16)


def pick(one_hot, x):
    both = jnp.dot(one_hot, jnp.concatenate(split2(x), axis=1), preferred_element_type=F32)
    return both[:, :LANES] + both[:, LANES:]


def flipped(me, bits, size):
    out, step = me * 0, 1
    while step < size:
        out += ((me // step + bits // step) % 2) * step
        step *= 2
    return out


def peers_of(me, size):
    if size & (size - 1):
        return [lax.rem(me + o, size) for o in range(1, size)]
    return [flipped(me, bits, size) for bits in range(size - 1, 0, -1)]


def kernel(
    n_row, n_col, total,
    s_hbm, e_hbm, t_hbm, tr_hbm, tc_hbm, cnt_hbm,
    out_ref,
    s_ref, e_ref, tr_ref, tc_ref, cnt_ref, t_ref, w_ref, rowbuf, colbuf, dfull, mfull, drecv, mrecv,
    pay, s1buf, s2buf, paya, buf3,
    oc, orr, oct_, ort, tt, xb, xa, dt,
    in_sem, gc_s, gc_r, gr_s, gr_r, rd_s, rd_r, rm_s, rm_r,
    a1_s, a1_r, a2_s, a2_r, a3_s, a3_r,
):
    r = lax.axis_index("row")
    c = lax.axis_index("col")
    pr = s_ref.shape[0]
    slots = t_ref.shape[0]
    flat = t_ref.shape[1]
    part = flat // LOADS

    load_s, load_tr, load_tc, load_cnt, load_e = loads = [
        pltpu.make_async_copy(src, dst, in_sem.at[i])
        for i, (src, dst) in enumerate([
            (s_hbm, s_ref), (tr_hbm, tr_ref), (tc_hbm, tc_ref),
            (cnt_hbm, cnt_ref), (e_hbm, e_ref),
        ])
    ]
    load_t = []
    for i in range(LOADS):
        cols = pl.ds(i * part, part)
        load_t.append(pltpu.make_async_copy(t_hbm.at[:, cols], t_ref.at[:, cols], in_sem.at[len(loads) + i]))
    for d in loads + load_t:
        d.start()

    row_peers = peers_of(r, n_row)
    col_peers = peers_of(c, n_col)

    barrier = pltpu.get_barrier_semaphore()
    for p in row_peers:
        pl.semaphore_signal(barrier, inc=1, device_id=(p, c), device_id_type=MESH)
    for p in col_peers:
        pl.semaphore_signal(barrier, inc=1, device_id=(r, p), device_id_type=MESH)
    pl.semaphore_wait(barrier, n_row + n_col - 2)

    def remote(src, dst, ss, rs, dev):
        return pltpu.make_async_remote_copy(
            src_ref=src, dst_ref=dst, send_sem=ss, recv_sem=rs,
            device_id=dev, device_id_type=MESH,
        )

    def slab(p):
        return pl.ds(pl.multiple_of(p * pr, pr), pr)

    sends = []
    near = (row_peers[0], c)

    def spread_out(copies, span, ss, rs):
        for src, dst, dev in copies:
            remote(src, dst, ss, rs, dev).start()
        sends.append(remote(span, span, ss, rs, near))

    def all_in(span, ss, rs):
        remote(span, span, ss, rs, near).wait_recv()

    def col_span(it):
        return colbuf.at[it, pl.ds(0, (n_row - 1) * pr)]

    def row_span(it):
        return rowbuf.at[it, pl.ds(0, (n_col - 1) * pr)]

    def gather(it, src):
        spread_out([(src, colbuf.at[it, slab(r)], (p, c)) for p in row_peers], col_span(it), gc_s.at[it], gc_r.at[it])
        spread_out([(src, rowbuf.at[it, slab(c)], (r, p)) for p in col_peers], row_span(it), gr_s.at[it], gr_r.at[it])

    def wait_col(it):
        all_in(col_span(it), gc_s.at[it], gc_r.at[it])

    def wait_row(it):
        all_in(row_span(it), gr_s.at[it], gr_r.at[it])

    def scal_one(k):
        spread_out(
            [(pay.at[k, 0], s1buf.at[k, r], (p, c)) for p in row_peers],
            s1buf.at[k, pl.ds(0, n_row - 1)], a1_s.at[k], a1_r.at[k],
        )

    def scal_one_get(k):
        all_in(s1buf.at[k, pl.ds(0, n_row - 1)], a1_s.at[k], a1_r.at[k])
        return [pay[k, 0]] + [s1buf[k, p] for p in row_peers]

    def scal_two(k):
        spread_out(
            [(pay.at[k, 1], s2buf.at[k, c], (r, p)) for p in col_peers],
            s2buf.at[k, pl.ds(0, n_col - 1)], a2_s.at[k], a2_r.at[k],
        )

    def scal_two_get(k):
        all_in(s2buf.at[k, pl.ds(0, n_col - 1)], a2_s.at[k], a2_r.at[k])
        return [pay[k, 1]] + [s2buf[k, p] for p in col_peers]

    def whole(x):
        return jnp.broadcast_to(jnp.sum(jnp.sum(x, axis=0, keepdims=True), axis=1, keepdims=True), (1, LANES))

    def moments(v, w):
        vw = whole(v * w)
        vv = whole(v * v)
        mean = jnp.where(vv > 0, vw / jnp.where(vv > 0, vv, 1.0), 0.0)
        z = w - mean * v
        return packed(vw, vv, whole(z * z), mean)

    def packed(vw, vv, zz, mean):
        return jnp.concatenate([vw, vv, zz, mean, jnp.zeros((4, LANES), F32)], axis=0)

    def spread_about(parts, center):
        out = jnp.zeros((1, LANES), F32)
        for q in parts:
            gap = center - q[3:4]
            out += q[2:3] + gap * gap * q[1:2]
        return out

    def merge(parts):
        vw = functools.reduce(jnp.add, [q[0:1] for q in parts])
        vv = functools.reduce(jnp.add, [q[1:2] for q in parts])
        mean = jnp.where(vv > 0, vw / jnp.where(vv > 0, vv, 1.0), 0.0)
        return packed(vw, vv, spread_about(parts, mean), mean)

    def alpha_beta(parts):
        vw = functools.reduce(jnp.add, [q[0:1] for q in parts])
        alpha = vw / total
        beta = jnp.sqrt(spread_about(parts, alpha) / total + 1e-06)
        return alpha, beta

    load_s.wait()
    s = s_ref[...]
    gather(0, s_ref)
    colbuf[0, slab(r)] = s
    rowbuf[0, slab(c)] = s
    pay[0, 0] = jnp.broadcast_to(whole(s * s), (8, LANES))
    scal_one(0)

    lane = lax.broadcasted_iota(jnp.int32, (slots, LANES), 1)
    load_cnt.wait()
    load_tr.wait()
    load_tc.wait()
    live = lax.broadcasted_iota(jnp.int32, (TILE, slots), 1) < cnt_ref[0, 0]
    a_row = tr_ref[...]
    b_row = tc_ref[...]
    a_col = jnp.transpose(jnp.broadcast_to(a_row, (LANES, slots)))
    b_col = jnp.transpose(jnp.broadcast_to(b_row, (LANES, slots)))

    def as_one(m):
        return jnp.where(m, 1.0, 0.0).astype(F32)

    for h in range(orr.shape[1] // LANES):
        orr[:, h * LANES:(h + 1) * LANES] = as_one((a_col >> 1) == lane + h * LANES).astype(BF16)
    for h in range(oc.shape[1] // LANES):
        oc[:, h * LANES:(h + 1) * LANES] = as_one((b_col >> 1) == lane + h * LANES).astype(BF16)
    ort[...] = as_one(jnp.broadcast_to(a_row >> 1, ort.shape) == lax.broadcasted_iota(jnp.int32, ort.shape, 0)).astype(BF16)
    oct_[...] = as_one(jnp.broadcast_to(b_row >> 1, oct_.shape) == lax.broadcasted_iota(jnp.int32, oct_.shape, 0)).astype(BF16)

    a_odd = jnp.broadcast_to(a_row & 1, (TILE, slots)) == 1
    b_odd = jnp.broadcast_to(b_row & 1, (TILE, slots)) == 1

    for i in range(flat // LANES):
        if i * LANES % part == 0:
            load_t[i * LANES // part].wait()
        cols = slice(i * LANES, (i + 1) * LANES)
        tt[cols, :] = jnp.transpose(t_ref[:, cols])

    def gathered(one_hot, x, odd):
        g = jnp.transpose(pick(one_hot, x))
        return jnp.where(odd, g[TILE:], g[:TILE])

    def scattered(one_hot, y, odd):
        zero = jnp.zeros_like(y)
        even_part = jnp.where(odd, zero, jnp.where(live, y, zero))
        odd_part = jnp.where(odd, jnp.where(live, y, zero), zero)
        both = lax.dot_general(
            one_hot, jnp.concatenate(split2(jnp.concatenate([even_part, odd_part], axis=0)), axis=0),
            (((1,), (1,)), ((), ())), preferred_element_type=F32,
        )
        return both[:, :LANES] + both[:, LANES:]

    sub = lax.broadcasted_iota(jnp.int32, (SUBLANES, slots), 0)

    def fold(parts):
        shift = 1
        while len(parts) > 1:
            low = (sub & shift) == 0
            parts = [
                jnp.where(low, p, q) + pltpu.roll(jnp.where(low, q, p), shift, 0)
                for p, q in zip(parts[::2], parts[1::2])
            ]
            shift *= 2
        return parts[0]

    def direct(it):
        xb[...] = gathered(oc[...], colbuf[it], b_odd)
        for g in range(TILE // SUBLANES):
            parts = []
            for a in range(g * SUBLANES, (g + 1) * SUBLANES):
                terms = [
                    tt[a * TILE + q:a * TILE + q + SUBLANES, :] * xb[q:q + SUBLANES, :]
                    for q in range(0, TILE, SUBLANES)
                ]
                parts.append(functools.reduce(jnp.add, terms))
            dt[g * SUBLANES:(g + 1) * SUBLANES, :] = fold(parts)
        dfull[it] = scattered(ort[...], dt[...], a_odd)
        spread_out(
            [(dfull.at[it, slab(p)], drecv.at[it, c], (r, p)) for p in col_peers],
            drecv.at[it, pl.ds(0, n_col - 1)], rd_s.at[it], rd_r.at[it],
        )

    def mirror(it):
        xa[...] = gathered(orr[...], rowbuf[it], a_odd)
        m = jnp.zeros((TILE, slots), F32)
        for a in range(TILE):
            m += tt[a * TILE:(a + 1) * TILE, :] * xa[a:a + 1, :]
        mfull[it] = scattered(oct_[...], m, b_odd)
        spread_out(
            [(mfull.at[it, slab(p)], mrecv.at[it, r], (p, c)) for p in row_peers],
            mrecv.at[it, pl.ds(0, n_row - 1)], rm_s.at[it], rm_r.at[it],
        )

    def collect(it, x):
        h = e_ref[...] * x + dfull[it, slab(c)] + mfull[it, slab(r)]
        all_in(drecv.at[it, pl.ds(0, n_col - 1)], rd_s.at[it], rd_r.at[it])
        for p in col_peers:
            h += drecv[it, p]
        all_in(mrecv.at[it, pl.ds(0, n_row - 1)], rm_s.at[it], rm_r.at[it])
        for p in row_peers:
            h += mrecv[it, p]
        return h

    load_e.wait()
    wait_col(0)
    direct(0)
    parts = scal_one_get(0)
    pay[0, 1] = functools.reduce(jnp.add, parts)
    scal_two(0)
    wait_row(0)
    mirror(0)
    square = functools.reduce(jnp.add, scal_two_get(0))[0:1]
    norm = jnp.sqrt(square / total + 1e-06)
    v0 = s / norm
    w0 = collect(0, s) / norm
    w_ref[...] = w0
    gather(1, w_ref)
    colbuf[1, slab(r)] = w0
    rowbuf[1, slab(c)] = w0
    pay[1, 0] = moments(v0, w0)
    scal_one(1)
    wait_col(1)
    direct(1)
    pay[1, 1] = merge(scal_one_get(1))
    scal_two(1)
    wait_row(1)
    mirror(1)
    alpha0, beta0 = alpha_beta(scal_two_get(1))
    v1 = (w0 - alpha0 * v0) / beta0
    w1 = (collect(1, w0) - alpha0 * w0) / beta0 - beta0 * v0
    at = lax.broadcasted_iota(jnp.int32, (1, LANES), 1)
    quarter = at // (LANES // 4)

    def part(x, q):
        return jnp.where(quarter == q, x, 0.0)

    def share(x):
        x = x + pltpu.roll(x, LANES // 4, 1)
        return x + pltpu.roll(x, LANES // 2, 1)

    mine = moments(v1, w1)
    me = r * n_col + c
    count = n_row * n_col
    row = part(mine[0:1], 0) + part(mine[2:3], 1) + part(mine[1:2], 2) + part(mine[3:4], 3)
    buf3[me] = row
    paya[...] = row
    others = [(p, q) for p in row_peers + [r] for q in col_peers + [c]][:-1]
    span = buf3.at[pl.ds(0, count - 1)]
    for p, q in others:
        remote(paya, buf3.at[me], a3_s, a3_r, (p, q)).start()
    for d in sends:
        d.wait_send()
    all_in(span, a3_s, a3_r)
    rows = [buf3[i] for i in range(count)]
    total_row = functools.reduce(jnp.add, rows)
    alpha1 = share(part(total_row, 0)) / total
    gaps = functools.reduce(
        jnp.add, [(alpha1 - q) * (alpha1 - q) * pltpu.roll(q, LANES // 4, 1) for q in rows]
    )
    beta1 = jnp.sqrt(share(part(gaps, 3) + part(total_row, 1)) / total + 1e-06)
    out_ref[:pr] = (w1 - alpha1 * v1) / beta1
    out_ref[pr:] = jnp.concatenate(
        [jnp.where(at == 0, alpha0, alpha1), jnp.where(at == 0, beta0, beta1), jnp.zeros((6, LANES), F32)], axis=0
    )
    remote(span, span, a3_s, a3_r, near).wait_send()


def hand_out(in_ref, vec_ref, al_ref, be_ref):
    pr = vec_ref.shape[0]
    vec_ref[...] = in_ref[:pr]
    al_ref[...] = in_ref[pr, :STEPS]
    be_ref[...] = in_ref[pr + 1, :STEPS]


def local(start_vector, energies, tile_values, tile_rows, tile_cols, tile_counts):
    n_row = lax.axis_size("row")
    n_col = lax.axis_size("col")
    piece = start_vector.shape[0]
    pr = piece // LANES
    slots, flat = tile_values.shape[1:]
    rr, cr = n_col * pr, n_row * pr
    vm = pl.BlockSpec(memory_space=pltpu.VMEM)
    dma = pltpu.SemaphoreType.DMA
    out = pl.pallas_call(
        functools.partial(kernel, n_row, n_col, float(piece * n_row * n_col)),
        out_shape=pltpu.VMEM((pr + 8, LANES), F32),
        in_specs=[pl.BlockSpec(memory_space=pltpu.HBM)] * 6,
        out_specs=vm,
        scratch_shapes=[
            pltpu.VMEM((pr, LANES), F32),
            pltpu.VMEM((pr, LANES), F32),
            pltpu.VMEM(tile_rows.shape, jnp.int32),
            pltpu.VMEM(tile_cols.shape, jnp.int32),
            pltpu.SMEM(tile_counts.shape, jnp.int32),
            pltpu.VMEM((slots, flat), F32),
            pltpu.VMEM((pr, LANES), F32),
            pltpu.VMEM((2, rr, LANES), F32),
            pltpu.VMEM((2, cr, LANES), F32),
            pltpu.VMEM((2, rr, LANES), F32),
            pltpu.VMEM((2, cr, LANES), F32),
            pltpu.VMEM((2, n_col, pr, LANES), F32),
            pltpu.VMEM((2, n_row, pr, LANES), F32),
            pltpu.VMEM((2, 2, 8, LANES), F32),
            pltpu.VMEM((2, n_row, 8, LANES), F32),
            pltpu.VMEM((2, n_col, 8, LANES), F32),
            pltpu.VMEM((1, LANES), F32),
            pltpu.VMEM((n_row * n_col, 1, LANES), F32),
            pltpu.VMEM((slots, cr), BF16),
            pltpu.VMEM((slots, rr), BF16),
            pltpu.VMEM((cr, slots), BF16),
            pltpu.VMEM((rr, slots), BF16),
            pltpu.VMEM((flat, slots), F32),
            pltpu.VMEM((TILE, slots), F32),
            pltpu.VMEM((TILE, slots), F32),
            pltpu.VMEM((TILE, slots), F32),
            dma((5 + LOADS,)),
            *[dma((2,))] * 12,
            dma(()), dma(()),
        ],
        compiler_params=pltpu.CompilerParams(
            collective_id=0, has_side_effects=True, vmem_limit_bytes=60000000
        ),
    )(
        start_vector.reshape(pr, LANES),
        energies.reshape(pr, LANES),
        tile_values.reshape(slots, flat),
        tile_rows,
        tile_cols,
        tile_counts,
    )
    vector, alphas, betas = pl.pallas_call(
        hand_out,
        out_shape=(
            jax.ShapeDtypeStruct((pr, LANES), F32),
            jax.ShapeDtypeStruct((STEPS,), F32),
            jax.ShapeDtypeStruct((STEPS,), F32),
        ),
        in_specs=[vm],
        out_specs=(vm, vm, vm),
        compiler_params=pltpu.CompilerParams(vmem_limit_bytes=1048576),
    )(out)
    return vector.reshape(piece), alphas, betas


def solution(mesh):
    placed = (
        P(("row", "col")),
        P(("row", "col")),
        P("row", "col", None),
        P("row", "col"),
        P("row", "col"),
        P("row", "col"),
    )
    return jax.shard_map(
        local, mesh=mesh, in_specs=placed, out_specs=(P(("row", "col")), P(), P()), check_vma=False
    )
```

```python
import functools

import jax
import jax.numpy as jnp
from jax import lax
from jax.experimental import pallas as pl
from jax.experimental.pallas import tpu as pltpu
from jax.sharding import PartitionSpec as P

TILE = 64
STEPS = 2
LANES = 128
LOADS = 4
SUBLANES = 8
MESH = pl.DeviceIdType.MESH
F32 = jnp.float32
BF16 = jnp.bfloat16


def split2(x):
    hi = x.astype(BF16)
    return hi, (x - hi.astype(F32)).astype(BF16)


def pick(one_hot, x):
    both = jnp.dot(one_hot, jnp.concatenate(split2(x), axis=1), preferred_element_type=F32)
    return both[:, :LANES] + both[:, LANES:]


def flipped(me, bits, size):
    out, step = me * 0, 1
    while step < size:
        out += ((me // step + bits // step) % 2) * step
        step *= 2
    return out


def peers_of(me, size):
    if size & (size - 1):
        return [lax.rem(me + o, size) for o in range(1, size)]
    return [flipped(me, bits, size) for bits in range(size - 1, 0, -1)]


def kernel(
    n_row, n_col, total,
    s_hbm, e_hbm, t_hbm, tr_hbm, tc_hbm, cnt_hbm,
    out_ref,
    s_ref, e_ref, tr_ref, tc_ref, cnt_ref, t_ref, w_ref, rowbuf, colbuf, dfull, mfull, drecv, mrecv,
    pay, s1buf, s2buf, paya, buf3,
    oc, orr, oct_, ort, tt, xb, xa, dt,
    in_sem, gc_s, gc_r, gr_s, gr_r, rd_s, rd_r, rm_s, rm_r,
    a1_s, a1_r, a2_s, a2_r, a3_s, a3_r, g0_s, g0_r,
):
    r = lax.axis_index("row")
    c = lax.axis_index("col")
    pr = s_ref.shape[0]
    slots = t_ref.shape[0]
    flat = t_ref.shape[1]
    part = flat // LOADS

    load_s, load_tr, load_tc, load_cnt, load_e = loads = [
        pltpu.make_async_copy(src, dst, in_sem.at[i])
        for i, (src, dst) in enumerate([
            (s_hbm, s_ref), (tr_hbm, tr_ref), (tc_hbm, tc_ref),
            (cnt_hbm, cnt_ref), (e_hbm, e_ref),
        ])
    ]
    load_t = []
    for i in range(LOADS):
        cols = pl.ds(i * part, part)
        load_t.append(pltpu.make_async_copy(t_hbm.at[:, cols], t_ref.at[:, cols], in_sem.at[len(loads) + i]))
    for d in loads + load_t:
        d.start()

    row_peers = peers_of(r, n_row)
    col_peers = peers_of(c, n_col)

    barrier = pltpu.get_barrier_semaphore()
    for p in row_peers:
        pl.semaphore_signal(barrier, inc=1, device_id=(p, c), device_id_type=MESH)
    above = [(o, c + o, c + o < n_col) for o in range(1, n_col)]
    below = [(o, c - o, c >= o) for o in range(1, n_col)]
    has_next = c + 1 < n_col

    def greet(p):
        pl.semaphore_signal(barrier, inc=1, device_id=(r, p), device_id_type=MESH)

    for o, p, there in above:
        pl.when(there)(functools.partial(greet, p))
    pl.when(c >= 1)(functools.partial(greet, c - 1))
    pl.semaphore_wait(barrier, n_row - 1 + c + lax.rem(jnp.minimum(c + 1, n_col - 1) + n_col - c, n_col))

    def remote(src, dst, ss, rs, dev):
        return pltpu.make_async_remote_copy(
            src_ref=src, dst_ref=dst, send_sem=ss, recv_sem=rs,
            device_id=dev, device_id_type=MESH,
        )

    def slab(p):
        return pl.ds(pl.multiple_of(p * pr, pr), pr)

    sends = []
    near = (row_peers[0], c)

    def spread_out(copies, span, ss, rs):
        for src, dst, dev in copies:
            remote(src, dst, ss, rs, dev).start()
        sends.append(remote(span, span, ss, rs, near))

    def all_in(span, ss, rs):
        remote(span, span, ss, rs, near).wait_recv()

    def col_span(it):
        return colbuf.at[it, pl.ds(0, (n_row - 1) * pr)]

    def row_span(it):
        return rowbuf.at[it, pl.ds(0, (n_col - 1) * pr)]

    def piece(k, ss, p):
        return remote(rowbuf.at[0, slab(k)], rowbuf.at[0, slab(k)], ss, g0_r.at[k], (r, p))

    def own(ss, p):
        return remote(s_ref, rowbuf.at[0, slab(c)], ss, g0_r.at[c], (r, p))

    def first_gather():
        gather_col(0, s_ref)
        for o, p, there in reversed(below):
            pl.when(there)(lambda o=o, p=p: own(g0_s.at[o], p).start())
        pl.when(has_next)(lambda: own(g0_s.at[0], c + 1).start())

    def pass_on():
        for o, k, there in below:
            pl.when(there)(lambda k=k: piece(k, g0_s.at[0], k).wait_recv())
            pl.when(jnp.logical_and(there, has_next))(lambda o=o, k=k: piece(k, g0_s.at[n_col + o], c + 1).start())

    def first_row():
        for o, k, there in above:
            pl.when(there)(lambda k=k: piece(k, g0_s.at[0], k).wait_recv())

    def first_sent():
        for o, k, there in below:
            pl.when(there)(lambda o=o, k=k: own(g0_s.at[o], k).wait_send())
            pl.when(jnp.logical_and(there, has_next))(lambda o=o, k=k: piece(k, g0_s.at[n_col + o], c + 1).wait_send())
        pl.when(has_next)(lambda: own(g0_s.at[0], c + 1).wait_send())

    def gather_col(it, src):
        spread_out([(src, colbuf.at[it, slab(r)], (p, c)) for p in row_peers], col_span(it), gc_s.at[it], gc_r.at[it])

    def gather(it, src):
        gather_col(it, src)
        spread_out([(src, rowbuf.at[it, slab(c)], (r, p)) for p in col_peers], row_span(it), gr_s.at[it], gr_r.at[it])

    def wait_col(it):
        all_in(col_span(it), gc_s.at[it], gc_r.at[it])

    def wait_row(it):
        all_in(row_span(it), gr_s.at[it], gr_r.at[it])

    def scal_one(k):
        spread_out(
            [(pay.at[k, 0], s1buf.at[k, r], (p, c)) for p in row_peers],
            s1buf.at[k, pl.ds(0, n_row - 1)], a1_s.at[k], a1_r.at[k],
        )

    def scal_one_get(k):
        all_in(s1buf.at[k, pl.ds(0, n_row - 1)], a1_s.at[k], a1_r.at[k])
        return [pay[k, 0]] + [s1buf[k, p] for p in row_peers]

    def scal_two(k):
        spread_out(
            [(pay.at[k, 1], s2buf.at[k, c], (r, p)) for p in col_peers],
            s2buf.at[k, pl.ds(0, n_col - 1)], a2_s.at[k], a2_r.at[k],
        )

    def scal_two_get(k):
        all_in(s2buf.at[k, pl.ds(0, n_col - 1)], a2_s.at[k], a2_r.at[k])
        return [pay[k, 1]] + [s2buf[k, p] for p in col_peers]

    def whole(x):
        return jnp.broadcast_to(jnp.sum(jnp.sum(x, axis=0, keepdims=True), axis=1, keepdims=True), (1, LANES))

    def moments(v, w):
        vw = whole(v * w)
        vv = whole(v * v)
        mean = jnp.where(vv > 0, vw / jnp.where(vv > 0, vv, 1.0), 0.0)
        z = w - mean * v
        return packed(vw, vv, whole(z * z), mean)

    def packed(vw, vv, zz, mean):
        return jnp.concatenate([vw, vv, zz, mean, jnp.zeros((4, LANES), F32)], axis=0)

    def spread_about(parts, center):
        out = jnp.zeros((1, LANES), F32)
        for q in parts:
            gap = center - q[3:4]
            out += q[2:3] + gap * gap * q[1:2]
        return out

    def merge(parts):
        vw = functools.reduce(jnp.add, [q[0:1] for q in parts])
        vv = functools.reduce(jnp.add, [q[1:2] for q in parts])
        mean = jnp.where(vv > 0, vw / jnp.where(vv > 0, vv, 1.0), 0.0)
        return packed(vw, vv, spread_about(parts, mean), mean)

    def alpha_beta(parts):
        vw = functools.reduce(jnp.add, [q[0:1] for q in parts])
        alpha = vw / total
        beta = jnp.sqrt(spread_about(parts, alpha) / total + 1e-06)
        return alpha, beta

    load_s.wait()
    s = s_ref[...]
    first_gather()
    colbuf[0, slab(r)] = s
    rowbuf[0, slab(c)] = s
    pay[0, 0] = jnp.broadcast_to(whole(s * s), (8, LANES))
    scal_one(0)

    lane = lax.broadcasted_iota(jnp.int32, (slots, LANES), 1)
    load_cnt.wait()
    load_tr.wait()
    load_tc.wait()
    live = lax.broadcasted_iota(jnp.int32, (TILE, slots), 1) < cnt_ref[0, 0]
    a_row = tr_ref[...]
    b_row = tc_ref[...]
    a_col = jnp.transpose(jnp.broadcast_to(a_row, (LANES, slots)))
    b_col = jnp.transpose(jnp.broadcast_to(b_row, (LANES, slots)))

    def as_one(m):
        return jnp.where(m, 1.0, 0.0).astype(F32)

    for h in range(orr.shape[1] // LANES):
        orr[:, h * LANES:(h + 1) * LANES] = as_one((a_col >> 1) == lane + h * LANES).astype(BF16)
    for h in range(oc.shape[1] // LANES):
        oc[:, h * LANES:(h + 1) * LANES] = as_one((b_col >> 1) == lane + h * LANES).astype(BF16)
    ort[...] = as_one(jnp.broadcast_to(a_row >> 1, ort.shape) == lax.broadcasted_iota(jnp.int32, ort.shape, 0)).astype(BF16)
    oct_[...] = as_one(jnp.broadcast_to(b_row >> 1, oct_.shape) == lax.broadcasted_iota(jnp.int32, oct_.shape, 0)).astype(BF16)

    a_odd = jnp.broadcast_to(a_row & 1, (TILE, slots)) == 1
    b_odd = jnp.broadcast_to(b_row & 1, (TILE, slots)) == 1

    for i in range(flat // LANES):
        if i * LANES % part == 0:
            load_t[i * LANES // part].wait()
        cols = slice(i * LANES, (i + 1) * LANES)
        tt[cols, :] = jnp.transpose(t_ref[:, cols])

    def gathered(one_hot, x, odd):
        g = jnp.transpose(pick(one_hot, x))
        return jnp.where(odd, g[TILE:], g[:TILE])

    def scattered(one_hot, y, odd):
        zero = jnp.zeros_like(y)
        even_part = jnp.where(odd, zero, jnp.where(live, y, zero))
        odd_part = jnp.where(odd, jnp.where(live, y, zero), zero)
        both = lax.dot_general(
            one_hot, jnp.concatenate(split2(jnp.concatenate([even_part, odd_part], axis=0)), axis=0),
            (((1,), (1,)), ((), ())), preferred_element_type=F32,
        )
        return both[:, :LANES] + both[:, LANES:]

    sub = lax.broadcasted_iota(jnp.int32, (SUBLANES, slots), 0)

    def fold(parts):
        shift = 1
        while len(parts) > 1:
            low = (sub & shift) == 0
            parts = [
                jnp.where(low, p, q) + pltpu.roll(jnp.where(low, q, p), shift, 0)
                for p, q in zip(parts[::2], parts[1::2])
            ]
            shift *= 2
        return parts[0]

    def direct(it):
        xb[...] = gathered(oc[...], colbuf[it], b_odd)
        for g in range(TILE // SUBLANES):
            parts = []
            for a in range(g * SUBLANES, (g + 1) * SUBLANES):
                terms = [
                    tt[a * TILE + q:a * TILE + q + SUBLANES, :] * xb[q:q + SUBLANES, :]
                    for q in range(0, TILE, SUBLANES)
                ]
                parts.append(functools.reduce(jnp.add, terms))
            dt[g * SUBLANES:(g + 1) * SUBLANES, :] = fold(parts)
        dfull[it] = scattered(ort[...], dt[...], a_odd)
        if it == 0:
            first_row()
        spread_out(
            [(dfull.at[it, slab(p)], drecv.at[it, c], (r, p)) for p in col_peers],
            drecv.at[it, pl.ds(0, n_col - 1)], rd_s.at[it], rd_r.at[it],
        )

    def mirror(it):
        xa[...] = gathered(orr[...], rowbuf[it], a_odd)
        m = jnp.zeros((TILE, slots), F32)
        for a in range(TILE):
            m += tt[a * TILE:(a + 1) * TILE, :] * xa[a:a + 1, :]
        mfull[it] = scattered(oct_[...], m, b_odd)
        spread_out(
            [(mfull.at[it, slab(p)], mrecv.at[it, r], (p, c)) for p in row_peers],
            mrecv.at[it, pl.ds(0, n_row - 1)], rm_s.at[it], rm_r.at[it],
        )

    def collect(it, x):
        h = e_ref[...] * x + dfull[it, slab(c)] + mfull[it, slab(r)]
        all_in(drecv.at[it, pl.ds(0, n_col - 1)], rd_s.at[it], rd_r.at[it])
        for p in col_peers:
            h += drecv[it, p]
        all_in(mrecv.at[it, pl.ds(0, n_row - 1)], rm_s.at[it], rm_r.at[it])
        for p in row_peers:
            h += mrecv[it, p]
        return h

    pass_on()
    load_e.wait()
    wait_col(0)
    direct(0)
    parts = scal_one_get(0)
    pay[0, 1] = functools.reduce(jnp.add, parts)
    scal_two(0)
    mirror(0)
    square = functools.reduce(jnp.add, scal_two_get(0))[0:1]
    norm = jnp.sqrt(square / total + 1e-06)
    v0 = s / norm
    w0 = collect(0, s) / norm
    w_ref[...] = w0
    gather(1, w_ref)
    colbuf[1, slab(r)] = w0
    rowbuf[1, slab(c)] = w0
    pay[1, 0] = moments(v0, w0)
    scal_one(1)
    wait_col(1)
    direct(1)
    pay[1, 1] = merge(scal_one_get(1))
    scal_two(1)
    wait_row(1)
    mirror(1)
    alpha0, beta0 = alpha_beta(scal_two_get(1))
    v1 = (w0 - alpha0 * v0) / beta0
    w1 = (collect(1, w0) - alpha0 * w0) / beta0 - beta0 * v0
    at = lax.broadcasted_iota(jnp.int32, (1, LANES), 1)
    quarter = at // (LANES // 4)

    def part(x, q):
        return jnp.where(quarter == q, x, 0.0)

    def share(x):
        x = x + pltpu.roll(x, LANES // 4, 1)
        return x + pltpu.roll(x, LANES // 2, 1)

    mine = moments(v1, w1)
    me = r * n_col + c
    count = n_row * n_col
    row = part(mine[0:1], 0) + part(mine[2:3], 1) + part(mine[1:2], 2) + part(mine[3:4], 3)
    buf3[me] = row
    paya[...] = row
    others = [(p, q) for p in row_peers + [r] for q in col_peers + [c]][:-1]
    span = buf3.at[pl.ds(0, count - 1)]
    for p, q in others:
        remote(paya, buf3.at[me], a3_s, a3_r, (p, q)).start()
    first_sent()
    for d in sends:
        d.wait_send()
    all_in(span, a3_s, a3_r)
    rows = [buf3[i] for i in range(count)]
    total_row = functools.reduce(jnp.add, rows)
    alpha1 = share(part(total_row, 0)) / total
    gaps = functools.reduce(
        jnp.add, [(alpha1 - q) * (alpha1 - q) * pltpu.roll(q, LANES // 4, 1) for q in rows]
    )
    beta1 = jnp.sqrt(share(part(gaps, 3) + part(total_row, 1)) / total + 1e-06)
    out_ref[:pr] = (w1 - alpha1 * v1) / beta1
    out_ref[pr:] = jnp.concatenate(
        [jnp.where(at == 0, alpha0, alpha1), jnp.where(at == 0, beta0, beta1), jnp.zeros((6, LANES), F32)], axis=0
    )
    remote(span, span, a3_s, a3_r, near).wait_send()


def hand_out(in_ref, vec_ref, al_ref, be_ref):
    pr = vec_ref.shape[0]
    vec_ref[...] = in_ref[:pr]
    al_ref[...] = in_ref[pr, :STEPS]
    be_ref[...] = in_ref[pr + 1, :STEPS]


def local(start_vector, energies, tile_values, tile_rows, tile_cols, tile_counts):
    n_row = lax.axis_size("row")
    n_col = lax.axis_size("col")
    piece = start_vector.shape[0]
    pr = piece // LANES
    slots, flat = tile_values.shape[1:]
    rr, cr = n_col * pr, n_row * pr
    vm = pl.BlockSpec(memory_space=pltpu.VMEM)
    dma = pltpu.SemaphoreType.DMA
    out = pl.pallas_call(
        functools.partial(kernel, n_row, n_col, float(piece * n_row * n_col)),
        out_shape=pltpu.VMEM((pr + 8, LANES), F32),
        in_specs=[pl.BlockSpec(memory_space=pltpu.HBM)] * 6,
        out_specs=vm,
        scratch_shapes=[
            pltpu.VMEM((pr, LANES), F32),
            pltpu.VMEM((pr, LANES), F32),
            pltpu.VMEM(tile_rows.shape, jnp.int32),
            pltpu.VMEM(tile_cols.shape, jnp.int32),
            pltpu.SMEM(tile_counts.shape, jnp.int32),
            pltpu.VMEM((slots, flat), F32),
            pltpu.VMEM((pr, LANES), F32),
            pltpu.VMEM((2, rr, LANES), F32),
            pltpu.VMEM((2, cr, LANES), F32),
            pltpu.VMEM((2, rr, LANES), F32),
            pltpu.VMEM((2, cr, LANES), F32),
            pltpu.VMEM((2, n_col, pr, LANES), F32),
            pltpu.VMEM((2, n_row, pr, LANES), F32),
            pltpu.VMEM((2, 2, 8, LANES), F32),
            pltpu.VMEM((2, n_row, 8, LANES), F32),
            pltpu.VMEM((2, n_col, 8, LANES), F32),
            pltpu.VMEM((1, LANES), F32),
            pltpu.VMEM((n_row * n_col, 1, LANES), F32),
            pltpu.VMEM((slots, cr), BF16),
            pltpu.VMEM((slots, rr), BF16),
            pltpu.VMEM((cr, slots), BF16),
            pltpu.VMEM((rr, slots), BF16),
            pltpu.VMEM((flat, slots), F32),
            pltpu.VMEM((TILE, slots), F32),
            pltpu.VMEM((TILE, slots), F32),
            pltpu.VMEM((TILE, slots), F32),
            dma((5 + LOADS,)),
            *[dma((2,))] * 12,
            dma(()), dma(()),
            dma((2 * n_col,)), dma((n_col,)),
        ],
        compiler_params=pltpu.CompilerParams(
            collective_id=0, has_side_effects=True, vmem_limit_bytes=60000000
        ),
    )(
        start_vector.reshape(pr, LANES),
        energies.reshape(pr, LANES),
        tile_values.reshape(slots, flat),
        tile_rows,
        tile_cols,
        tile_counts,
    )
    vector, alphas, betas = pl.pallas_call(
        hand_out,
        out_shape=(
            jax.ShapeDtypeStruct((pr, LANES), F32),
            jax.ShapeDtypeStruct((STEPS,), F32),
            jax.ShapeDtypeStruct((STEPS,), F32),
        ),
        in_specs=[vm],
        out_specs=(vm, vm, vm),
        compiler_params=pltpu.CompilerParams(vmem_limit_bytes=1048576),
    )(out)
    return vector.reshape(piece), alphas, betas


def solution(mesh):
    placed = (
        P(("row", "col")),
        P(("row", "col")),
        P("row", "col", None),
        P("row", "col"),
        P("row", "col"),
        P("row", "col"),
    )
    return jax.shard_map(
        local, mesh=mesh, in_specs=placed, out_specs=(P(("row", "col")), P(), P()), check_vma=False
    )
```

```python
import functools

import jax
import jax.numpy as jnp
from jax import lax
from jax.experimental import pallas as pl
from jax.experimental.pallas import tpu as pltpu
from jax.sharding import PartitionSpec as P

TILE = 64
STEPS = 2
LANES = 128
LOADS = 4
SUBLANES = 8
MESH = pl.DeviceIdType.MESH
F32 = jnp.float32
BF16 = jnp.bfloat16


def split2(x):
    hi = x.astype(BF16)
    return hi, (x - hi.astype(F32)).astype(BF16)


def pick(one_hot, x):
    both = jnp.dot(one_hot, jnp.concatenate(split2(x), axis=1), preferred_element_type=F32)
    return both[:, :LANES] + both[:, LANES:]


def flipped(me, bits, size):
    out, step = me * 0, 1
    while step < size:
        out += ((me // step + bits // step) % 2) * step
        step *= 2
    return out


def peers_of(me, size):
    if size & (size - 1):
        return [lax.rem(me + o, size) for o in range(1, size)]
    return [flipped(me, bits, size) for bits in range(size - 1, 0, -1)]


def kernel(
    n_row, n_col, total,
    s_hbm, e_hbm, t_hbm, tr_hbm, tc_hbm, cnt_hbm,
    out_ref,
    s_ref, e_ref, tr_ref, tc_ref, cnt_ref, t_ref, w_ref, rowbuf, colbuf, dfull, mfull, drecv, mrecv,
    pay, s1buf, s2buf, paya, buf3,
    oc, orr, oct_, ort, tt, xb, xa, dt,
    in_sem, gc_s, gc_r, gr_s, gr_r, rd_s, rd_r, rm_s, rm_r,
    a1_s, a1_r, a2_s, a2_r, a3_s, a3_r,
):
    r = lax.axis_index("row")
    c = lax.axis_index("col")
    pr = s_ref.shape[0]
    slots = t_ref.shape[0]
    flat = t_ref.shape[1]
    part = flat // LOADS

    load_s, load_tr, load_tc, load_cnt, load_e = loads = [
        pltpu.make_async_copy(src, dst, in_sem.at[i])
        for i, (src, dst) in enumerate([
            (s_hbm, s_ref), (tr_hbm, tr_ref), (tc_hbm, tc_ref),
            (cnt_hbm, cnt_ref), (e_hbm, e_ref),
        ])
    ]
    load_t = []
    for i in range(LOADS):
        cols = pl.ds(i * part, part)
        load_t.append(pltpu.make_async_copy(t_hbm.at[:, cols], t_ref.at[:, cols], in_sem.at[len(loads) + i]))
    for d in loads + load_t:
        d.start()

    row_peers = peers_of(r, n_row)
    col_peers = peers_of(c, n_col)

    barrier = pltpu.get_barrier_semaphore()
    for p in row_peers:
        pl.semaphore_signal(barrier, inc=1, device_id=(p, c), device_id_type=MESH)
    for p in col_peers:
        pl.semaphore_signal(barrier, inc=1, device_id=(r, p), device_id_type=MESH)
    pl.semaphore_wait(barrier, n_row + n_col - 2)

    def remote(src, dst, ss, rs, dev):
        return pltpu.make_async_remote_copy(
            src_ref=src, dst_ref=dst, send_sem=ss, recv_sem=rs,
            device_id=dev, device_id_type=MESH,
        )

    def slab(p):
        return pl.ds(pl.multiple_of(p * pr, pr), pr)

    sends = []
    near = (row_peers[0], c)

    def spread_out(copies, span, ss, rs):
        for src, dst, dev in copies:
            remote(src, dst, ss, rs, dev).start()
        sends.append(remote(span, span, ss, rs, near))

    def all_in(span, ss, rs):
        remote(span, span, ss, rs, near).wait_recv()

    def col_span(it):
        return colbuf.at[it, pl.ds(0, (n_row - 1) * pr)]

    def row_span(it):
        return rowbuf.at[it, pl.ds(0, (n_col - 1) * pr)]

    def gather(it, src):
        spread_out([(src, colbuf.at[it, slab(r)], (p, c)) for p in row_peers], col_span(it), gc_s.at[it], gc_r.at[it])
        spread_out([(src, rowbuf.at[it, slab(c)], (r, p)) for p in col_peers], row_span(it), gr_s.at[it], gr_r.at[it])

    def wait_col(it):
        all_in(col_span(it), gc_s.at[it], gc_r.at[it])

    def wait_row(it):
        all_in(row_span(it), gr_s.at[it], gr_r.at[it])

    def scal_one(k):
        spread_out(
            [(pay.at[k, 0], s1buf.at[k, r], (p, c)) for p in row_peers],
            s1buf.at[k, pl.ds(0, n_row - 1)], a1_s.at[k], a1_r.at[k],
        )

    def scal_one_get(k):
        all_in(s1buf.at[k, pl.ds(0, n_row - 1)], a1_s.at[k], a1_r.at[k])
        return [pay[k, 0]] + [s1buf[k, p] for p in row_peers]

    def scal_two(k):
        spread_out(
            [(pay.at[k, 1], s2buf.at[k, c], (r, p)) for p in col_peers],
            s2buf.at[k, pl.ds(0, n_col - 1)], a2_s.at[k], a2_r.at[k],
        )

    def scal_two_get(k):
        all_in(s2buf.at[k, pl.ds(0, n_col - 1)], a2_s.at[k], a2_r.at[k])
        return [pay[k, 1]] + [s2buf[k, p] for p in col_peers]

    def whole(x):
        return jnp.broadcast_to(jnp.sum(jnp.sum(x, axis=0, keepdims=True), axis=1, keepdims=True), (1, LANES))

    def moments(v, w):
        vw = whole(v * w)
        vv = whole(v * v)
        mean = jnp.where(vv > 0, vw / jnp.where(vv > 0, vv, 1.0), 0.0)
        z = w - mean * v
        return packed(vw, vv, whole(z * z), mean)

    def packed(vw, vv, zz, mean):
        return jnp.concatenate([vw, vv, zz, mean, jnp.zeros((4, LANES), F32)], axis=0)

    def spread_about(parts, center):
        out = jnp.zeros((1, LANES), F32)
        for q in parts:
            gap = center - q[3:4]
            out += q[2:3] + gap * gap * q[1:2]
        return out

    def merge(parts):
        vw = functools.reduce(jnp.add, [q[0:1] for q in parts])
        vv = functools.reduce(jnp.add, [q[1:2] for q in parts])
        mean = jnp.where(vv > 0, vw / jnp.where(vv > 0, vv, 1.0), 0.0)
        return packed(vw, vv, spread_about(parts, mean), mean)

    def alpha_beta(parts):
        vw = functools.reduce(jnp.add, [q[0:1] for q in parts])
        alpha = vw / total
        beta = jnp.sqrt(spread_about(parts, alpha) / total + 1e-06)
        return alpha, beta

    load_s.wait()
    s = s_ref[...]
    gather(0, s_ref)
    colbuf[0, slab(r)] = s
    rowbuf[0, slab(c)] = s
    pay[0, 0] = jnp.broadcast_to(whole(s * s), (8, LANES))
    scal_one(0)

    lane = lax.broadcasted_iota(jnp.int32, (slots, LANES), 1)
    load_cnt.wait()
    load_tr.wait()
    load_tc.wait()
    live = lax.broadcasted_iota(jnp.int32, (TILE, slots), 1) < cnt_ref[0, 0]
    a_row = tr_ref[...]
    b_row = tc_ref[...]
    a_col = jnp.transpose(jnp.broadcast_to(a_row, (LANES, slots)))
    b_col = jnp.transpose(jnp.broadcast_to(b_row, (LANES, slots)))

    def as_one(m):
        return jnp.where(m, 1.0, 0.0).astype(F32)

    for h in range(orr.shape[1] // LANES):
        orr[:, h * LANES:(h + 1) * LANES] = as_one((a_col >> 1) == lane + h * LANES).astype(BF16)
    for h in range(oc.shape[1] // LANES):
        oc[:, h * LANES:(h + 1) * LANES] = as_one((b_col >> 1) == lane + h * LANES).astype(BF16)
    ort[...] = as_one(jnp.broadcast_to(a_row >> 1, ort.shape) == lax.broadcasted_iota(jnp.int32, ort.shape, 0)).astype(BF16)
    oct_[...] = as_one(jnp.broadcast_to(b_row >> 1, oct_.shape) == lax.broadcasted_iota(jnp.int32, oct_.shape, 0)).astype(BF16)

    a_odd = jnp.broadcast_to(a_row & 1, (TILE, slots)) == 1
    b_odd = jnp.broadcast_to(b_row & 1, (TILE, slots)) == 1

    for i in range(flat // LANES):
        if i * LANES % part == 0:
            load_t[i * LANES // part].wait()
        cols = slice(i * LANES, (i + 1) * LANES)
        tt[cols, :] = jnp.transpose(t_ref[:, cols])

    def gathered(one_hot, x, odd):
        g = jnp.transpose(pick(one_hot, x))
        return jnp.where(odd, g[TILE:], g[:TILE])

    def scattered(one_hot, y, odd):
        zero = jnp.zeros_like(y)
        even_part = jnp.where(odd, zero, jnp.where(live, y, zero))
        odd_part = jnp.where(odd, jnp.where(live, y, zero), zero)
        both = lax.dot_general(
            one_hot, jnp.concatenate(split2(jnp.concatenate([even_part, odd_part], axis=0)), axis=0),
            (((1,), (1,)), ((), ())), preferred_element_type=F32,
        )
        return both[:, :LANES] + both[:, LANES:]

    sub = lax.broadcasted_iota(jnp.int32, (SUBLANES, slots), 0)

    def fold(parts):
        shift = 1
        while len(parts) > 1:
            low = (sub & shift) == 0
            parts = [
                jnp.where(low, p, q) + pltpu.roll(jnp.where(low, q, p), shift, 0)
                for p, q in zip(parts[::2], parts[1::2])
            ]
            shift *= 2
        return parts[0]

    def direct(it):
        xb[...] = gathered(oc[...], colbuf[it], b_odd)
        for g in range(TILE // SUBLANES):
            parts = []
            for a in range(g * SUBLANES, (g + 1) * SUBLANES):
                terms = [
                    tt[a * TILE + q:a * TILE + q + SUBLANES, :] * xb[q:q + SUBLANES, :]
                    for q in range(0, TILE, SUBLANES)
                ]
                parts.append(functools.reduce(jnp.add, terms))
            dt[g * SUBLANES:(g + 1) * SUBLANES, :] = fold(parts)

    def place_direct(it):
        dfull[it] = scattered(ort[...], dt[...], a_odd)

    def send_direct(it):
        spread_out(
            [(dfull.at[it, slab(p)], drecv.at[it, c], (r, p)) for p in col_peers],
            drecv.at[it, pl.ds(0, n_col - 1)], rd_s.at[it], rd_r.at[it],
        )

    def pick_row(it):
        xa[...] = gathered(orr[...], rowbuf[it], a_odd)

    def mirror(it):
        m = jnp.zeros((TILE, slots), F32)
        for a in range(TILE):
            m += tt[a * TILE:(a + 1) * TILE, :] * xa[a:a + 1, :]
        mfull[it] = scattered(oct_[...], m, b_odd)
        spread_out(
            [(mfull.at[it, slab(p)], mrecv.at[it, r], (p, c)) for p in row_peers],
            mrecv.at[it, pl.ds(0, n_row - 1)], rm_s.at[it], rm_r.at[it],
        )

    def collect(it, x):
        h = e_ref[...] * x + dfull[it, slab(c)] + mfull[it, slab(r)]
        all_in(drecv.at[it, pl.ds(0, n_col - 1)], rd_s.at[it], rd_r.at[it])
        for p in col_peers:
            h += drecv[it, p]
        all_in(mrecv.at[it, pl.ds(0, n_row - 1)], rm_s.at[it], rm_r.at[it])
        for p in row_peers:
            h += mrecv[it, p]
        return h

    load_e.wait()
    wait_col(0)
    direct(0)
    place_direct(0)
    send_direct(0)
    parts = scal_one_get(0)
    pay[0, 1] = functools.reduce(jnp.add, parts)
    scal_two(0)
    wait_row(0)
    pick_row(0)
    mirror(0)
    square = functools.reduce(jnp.add, scal_two_get(0))[0:1]
    norm = jnp.sqrt(square / total + 1e-06)
    v0 = s / norm
    w0 = collect(0, s) / norm
    w_ref[...] = w0
    gather(1, w_ref)
    colbuf[1, slab(r)] = w0
    rowbuf[1, slab(c)] = w0
    pay[1, 0] = moments(v0, w0)
    scal_one(1)
    wait_col(1)
    direct(1)
    wait_row(1)
    parts = scal_one_get(1)
    place_direct(1)
    pick_row(1)
    pay[1, 1] = merge(parts)
    send_direct(1)
    mirror(1)
    scal_two(1)
    alpha0, beta0 = alpha_beta(scal_two_get(1))
    v1 = (w0 - alpha0 * v0) / beta0
    w1 = (collect(1, w0) - alpha0 * w0) / beta0 - beta0 * v0
    at = lax.broadcasted_iota(jnp.int32, (1, LANES), 1)
    quarter = at // (LANES // 4)

    def part(x, q):
        return jnp.where(quarter == q, x, 0.0)

    def share(x):
        x = x + pltpu.roll(x, LANES // 4, 1)
        return x + pltpu.roll(x, LANES // 2, 1)

    mine = moments(v1, w1)
    me = r * n_col + c
    count = n_row * n_col
    row = part(mine[0:1], 0) + part(mine[2:3], 1) + part(mine[1:2], 2) + part(mine[3:4], 3)
    buf3[me] = row
    paya[...] = row
    others = [(p, q) for p in row_peers + [r] for q in col_peers + [c]][:-1]
    span = buf3.at[pl.ds(0, count - 1)]
    for p, q in others:
        remote(paya, buf3.at[me], a3_s, a3_r, (p, q)).start()
    for d in sends:
        d.wait_send()
    all_in(span, a3_s, a3_r)
    rows = [buf3[i] for i in range(count)]
    total_row = functools.reduce(jnp.add, rows)
    alpha1 = share(part(total_row, 0)) / total
    gaps = functools.reduce(
        jnp.add, [(alpha1 - q) * (alpha1 - q) * pltpu.roll(q, LANES // 4, 1) for q in rows]
    )
    beta1 = jnp.sqrt(share(part(gaps, 3) + part(total_row, 1)) / total + 1e-06)
    out_ref[:pr] = (w1 - alpha1 * v1) / beta1
    out_ref[pr:] = jnp.concatenate(
        [jnp.where(at == 0, alpha0, alpha1), jnp.where(at == 0, beta0, beta1), jnp.zeros((6, LANES), F32)], axis=0
    )
    remote(span, span, a3_s, a3_r, near).wait_send()


def hand_out(in_ref, vec_ref, al_ref, be_ref):
    pr = vec_ref.shape[0]
    vec_ref[...] = in_ref[:pr]
    al_ref[...] = in_ref[pr, :STEPS]
    be_ref[...] = in_ref[pr + 1, :STEPS]


def local(start_vector, energies, tile_values, tile_rows, tile_cols, tile_counts):
    n_row = lax.axis_size("row")
    n_col = lax.axis_size("col")
    piece = start_vector.shape[0]
    pr = piece // LANES
    slots, flat = tile_values.shape[1:]
    rr, cr = n_col * pr, n_row * pr
    vm = pl.BlockSpec(memory_space=pltpu.VMEM)
    dma = pltpu.SemaphoreType.DMA
    out = pl.pallas_call(
        functools.partial(kernel, n_row, n_col, float(piece * n_row * n_col)),
        out_shape=pltpu.VMEM((pr + 8, LANES), F32),
        in_specs=[pl.BlockSpec(memory_space=pltpu.HBM)] * 6,
        out_specs=vm,
        scratch_shapes=[
            pltpu.VMEM((pr, LANES), F32),
            pltpu.VMEM((pr, LANES), F32),
            pltpu.VMEM(tile_rows.shape, jnp.int32),
            pltpu.VMEM(tile_cols.shape, jnp.int32),
            pltpu.SMEM(tile_counts.shape, jnp.int32),
            pltpu.VMEM((slots, flat), F32),
            pltpu.VMEM((pr, LANES), F32),
            pltpu.VMEM((2, rr, LANES), F32),
            pltpu.VMEM((2, cr, LANES), F32),
            pltpu.VMEM((2, rr, LANES), F32),
            pltpu.VMEM((2, cr, LANES), F32),
            pltpu.VMEM((2, n_col, pr, LANES), F32),
            pltpu.VMEM((2, n_row, pr, LANES), F32),
            pltpu.VMEM((2, 2, 8, LANES), F32),
            pltpu.VMEM((2, n_row, 8, LANES), F32),
            pltpu.VMEM((2, n_col, 8, LANES), F32),
            pltpu.VMEM((1, LANES), F32),
            pltpu.VMEM((n_row * n_col, 1, LANES), F32),
            pltpu.VMEM((slots, cr), BF16),
            pltpu.VMEM((slots, rr), BF16),
            pltpu.VMEM((cr, slots), BF16),
            pltpu.VMEM((rr, slots), BF16),
            pltpu.VMEM((flat, slots), F32),
            pltpu.VMEM((TILE, slots), F32),
            pltpu.VMEM((TILE, slots), F32),
            pltpu.VMEM((TILE, slots), F32),
            dma((5 + LOADS,)),
            *[dma((2,))] * 12,
            dma(()), dma(()),
        ],
        compiler_params=pltpu.CompilerParams(
            collective_id=0, has_side_effects=True, vmem_limit_bytes=60000000
        ),
    )(
        start_vector.reshape(pr, LANES),
        energies.reshape(pr, LANES),
        tile_values.reshape(slots, flat),
        tile_rows,
        tile_cols,
        tile_counts,
    )
    vector, alphas, betas = pl.pallas_call(
        hand_out,
        out_shape=(
            jax.ShapeDtypeStruct((pr, LANES), F32),
            jax.ShapeDtypeStruct((STEPS,), F32),
            jax.ShapeDtypeStruct((STEPS,), F32),
        ),
        in_specs=[vm],
        out_specs=(vm, vm, vm),
        compiler_params=pltpu.CompilerParams(vmem_limit_bytes=1048576),
    )(out)
    return vector.reshape(piece), alphas, betas


def solution(mesh):
    placed = (
        P(("row", "col")),
        P(("row", "col")),
        P("row", "col", None),
        P("row", "col"),
        P("row", "col"),
        P("row", "col"),
    )
    return jax.shard_map(
        local, mesh=mesh, in_specs=placed, out_specs=(P(("row", "col")), P(), P()), check_vma=False
    )
```
